512 devices in a mesh: row: 16 (over y, core), col: 32 (over x, z).
Axes of the slice: x: 4, y: 8, z: 8, core: 2. Of those that a mesh axis runs over, the one named last changes fastest.
Arguments:
- positions: float32 [4, 4096, 4096], P(None, 'row', 'col'), may hold values from -2 to 2, as said below
Outputs:
- rotated: float32 [4, 4096, 4096], P(None, 'row', 'col')
The draws below stay inside these ranges and needn't reach their ends.
Inputs may be any that keep to these rules, and one draw needn't show every extreme that they name: `positions`: each of the 4 matrices is symmetric.
All inputs are finite; a program needn't handle non-finite values.
Results may differ from the reference program's by a relative error of at most 0.00026.
Values sent between devices are 32-bit elements; how exact they have to be, the bound alone decides.
A program may use at most 64 MiB of HBM per device.

```python
import jax
import jax.numpy as jnp
import numpy as np
from jax import lax

N = 4096
KMAT = 4
TERMS = 4
BLOCK = 128
N_COL = 32


def draw_positions(key, part):
    keys = jax.random.split(key, 3)
    spread = N ** (-0.5)
    raw = jax.random.truncated_normal(keys[0], -4.0, 4.0, (KMAT, N, N), jnp.float32)
    centres = jax.random.uniform(keys[2], (KMAT, N), jnp.float32, -1.5, 1.5)
    upper_part = jnp.triu(raw * spread, 1)
    identity = jnp.eye(N, dtype=jnp.float32)
    return upper_part + jnp.swapaxes(upper_part, 1, 2) + centres[:, :, None] * identity[None, :, :]


def setup_inputs(seed: int = 0) -> dict:
    arg_keys = jax.random.split(jax.random.key(seed), 2)
    return {
        "positions": draw_positions(jax.random.fold_in(arg_keys[1], 71), 0),
    }


STEP_SIZE = 0.4
HIGHEST = lax.Precision.HIGHEST


def pair_indices(stride):
    leaders = [first_block for first_block in range(N_COL) if first_block % (2 * stride) < stride]
    rows_of = []
    for first_block in leaders:
        lower_rows = np.arange(first_block * BLOCK, (first_block + 1) * BLOCK)
        upper_rows = np.arange((first_block + stride) * BLOCK, (first_block + stride + 1) * BLOCK)
        rows_of.append(np.concatenate([lower_rows, upper_rows]))
    return np.stack(rows_of).astype(np.int32)


def taylor_series(generator):
    pair_width = generator.shape[-1]
    identity = jnp.broadcast_to(jnp.eye(pair_width, dtype=generator.dtype), generator.shape)
    current = identity
    summed = identity
    for power in range(1, TERMS + 1):
        current = jnp.einsum('pij,pjk->pik', generator, current, precision=HIGHEST) / power
        summed = summed + current
    return summed


def jacobi_round(positions, stride):
    groups = pair_indices(stride)
    pair_count = groups.shape[0]
    pair_width = groups.shape[1]
    order_index = groups.reshape(-1)
    inverse_index = np.argsort(order_index).astype(np.int32)
    diagonal_blocks = positions[:, groups[:, :, None], groups[:, None, :]]
    centres = jnp.diagonal(diagonal_blocks, axis1=2, axis2=3)
    generator = STEP_SIZE * jnp.sum(diagonal_blocks * (centres[:, :, None, :] - centres[:, :, :, None]), axis=0)
    rotation = taylor_series(generator)
    results = []
    for matrix_id in range(KMAT):
        permuted = positions[matrix_id][order_index][:, order_index].reshape(pair_count, pair_width, pair_count, pair_width)
        left_side = jnp.einsum('pia,piqb->paqb', rotation, permuted, precision=HIGHEST)
        both_sides = jnp.einsum('paqj,qjb->paqb', left_side, rotation, precision=HIGHEST)
        results.append(both_sides.reshape(N, N)[inverse_index][:, inverse_index])
    return jnp.stack(results)


def reference(positions):
    round_positions = jacobi_round(positions, 1)
    return jacobi_round(round_positions, N_COL // 2)
```

```python
import functools

import jax
import jax.numpy as jnp
from jax import lax
from jax.experimental import pallas as pl
from jax.experimental.pallas import tpu as pltpu
from jax.sharding import PartitionSpec as P

STEP_SIZE = 0.4
B = 128
MESH = pl.DeviceIdType.MESH
F32 = jnp.float32
BF16 = jnp.bfloat16
REACH = {1: (0,), 2: (0, 1), 4: (2, 1, -1, 0)}


def split(value):
    high = value.astype(BF16)
    return high, (value - high.astype(F32)).astype(BF16)


def product(left, right):
    dot = functools.partial(jnp.dot, preferred_element_type=F32)
    return dot(left[0], right[0]) + (dot(left[0], right[1]) + dot(left[1], right[0]))


def block(index):
    return pl.ds(index * B, B)


def kernel(
    n_row,
    n_col,
    pos_ref,
    out_ref,
    quad,
    half_done,
    turned,
    parts,
    arrived,
    gen,
    full,
    rows_high,
    rows_low,
    cols_high,
    cols_low,
    done,
    landed,
    keep_sem,
    p_send,
    p_recv,
    y_send,
    y_recv,
    r_send,
    r_recv,
    a_send,
    a_recv,
    b_send,
    b_recv,
    z_send,
    z_recv,
):
    n_quad = n_col // 4
    row = lax.axis_index("row")
    col = lax.axis_index("col")
    row_quad, upper = lax.rem(row, n_quad), lax.div(row, n_quad)
    col_high, low = lax.div(col, n_col // 2), lax.rem(col, 2)
    col_quad = lax.div(lax.rem(col, n_col // 2), 2)
    mine = 2 * col_high + low
    on_diagonal = row_quad == col_quad
    off_diagonal = row_quad != col_quad
    far_row = lax.rem(row + n_quad, n_row)

    def column(quad_id, place):
        return (n_col // 2) * lax.div(place, 2) + 2 * quad_id + lax.rem(place, 2)

    def peer(step):
        place = lax.rem(mine + step, 4)
        return place, (row, column(col_quad, place))

    def sender(step):
        return lax.rem(mine + 4 - step, 4)

    def remote(src, dst, send, recv, device):
        return pltpu.make_async_remote_copy(
            src_ref=src, dst_ref=dst, send_sem=send, recv_sem=recv, device_id=device, device_id_type=MESH
        )

    reach = REACH[n_row // 4]
    row_targets = [(row, column(lax.rem(row_quad + hop, n_quad), mine)) for hop in range(1, n_quad)]
    chip, core = lax.div(row, 2), lax.rem(row, 2)
    col_targets = []
    for hop in reach:
        there = lax.rem(chip + n_row // 2 + hop, n_row // 2)
        col_targets.append((2 * there + 1 - core, col))
        if hop != 0:
            col_targets.append((2 * there + core, col))
    row_source = (row, column(row_quad, mine))
    away = lax.rem(chip + n_row // 2 - lax.div(col_quad, 2), n_row // 2)
    wraps = lax.div(away + n_row // 8 - (1 if n_row >= 16 else 0), n_row // 4) if n_row >= 16 else lax.div(away, n_row // 4)
    col_source = (lax.rem(col_quad + n_quad * lax.rem(wraps, 2), n_row), col)

    barrier = pltpu.get_barrier_semaphore()
    for step in (1, 2, 3):
        pl.semaphore_signal(barrier, inc=1, device_id=(row, column(col_quad, sender(step))), device_id_type=MESH)
    pl.semaphore_signal(barrier, inc=1, device_id=(far_row, col), device_id_type=MESH)

    @pl.when(off_diagonal)
    def _():
        pl.semaphore_signal(barrier, inc=1, device_id=row_source, device_id_type=MESH)
        pl.semaphore_signal(barrier, inc=1, device_id=col_source, device_id_type=MESH)
        pl.semaphore_wait(barrier, 4)

    @pl.when(on_diagonal)
    def _():
        pl.semaphore_wait(barrier, 4 + len(row_targets) + len(col_targets))

    own_rows = pl.ds(pl.multiple_of(upper * 2 * B, 2 * B), 2 * B)
    far_rows = pl.ds(pl.multiple_of((1 - upper) * 2 * B, 2 * B), 2 * B)

    def lanes(place):
        return pl.ds(pl.multiple_of(place * B, B), B)

    def share(step):
        place, device = peer(step)
        return remote(
            pos_ref.at[place], quad.at[own_rows, lanes(mine)], p_send.at[step - 1], p_recv.at[step - 1], device
        )

    for step in (3, 2, 1):
        share(step).start()
    keep = pltpu.make_async_copy(pos_ref.at[mine], quad.at[own_rows, lanes(mine)], keep_sem)
    keep.start()
    for step in (1, 2, 3):
        _, device = peer(step)
        remote(
            pos_ref.at[0], quad.at[own_rows, lanes(sender(step))], p_send.at[step - 1], p_recv.at[step - 1], device
        ).wait_recv()
    keep.wait()

    def cross(part):
        side = upper if part == 0 else 1 - upper
        view = quad.at[own_rows, pl.ds(pl.multiple_of(side * 2 * B, 2 * B), 2 * B)]
        return remote(view, view, y_send.at[part], y_recv.at[part], (far_row, col))

    def crossed(part):
        side = 1 - upper if part == 0 else upper
        view = quad.at[far_rows, pl.ds(pl.multiple_of(side * 2 * B, 2 * B), 2 * B)]
        return remote(view, view, y_send.at[part], y_recv.at[part], (far_row, col))

    cross(0).start()
    cross(1).start()

    row_ids = lax.broadcasted_iota(jnp.int32, (B, B), 0)
    col_ids = lax.broadcasted_iota(jnp.int32, (B, B), 1)

    def reduce_copy(turn, step):
        place, device = peer(step)
        return remote(
            parts.at[turn, place],
            arrived.at[turn, step - 1],
            r_send.at[turn, step - 1],
            r_recv.at[turn, step - 1],
            device,
        )

    def serve_copy(turn, number):
        if number < len(row_targets):
            kind, device = 0, row_targets[number]
        else:
            kind, device = 1, col_targets[number - len(row_targets)]
        return remote(
            gen.at[turn, 0, mine], gen.at[turn, kind, mine], a_send.at[turn, number], a_recv.at[turn, kind], device
        )

    def gather_copy(turn, kind, step):
        _, device = peer(step)
        return remote(
            gen.at[turn, kind, mine],
            gen.at[turn, kind, mine],
            b_send.at[turn, kind, step - 1],
            b_recv.at[turn, kind, step - 1],
            device,
        )

    def gather_wait(turn, kind, step):
        place = sender(step)
        _, device = peer(step)
        remote(
            gen.at[turn, kind, place],
            gen.at[turn, kind, place],
            b_send.at[turn, kind, step - 1],
            b_recv.at[turn, kind, step - 1],
            device,
        ).wait_recv()

    def make_parts(source, turn):
        for pair in (0, 1):
            first, second = block(2 * pair), block(2 * pair + 1)
            head, tail = source[first, first], source[second, second]
            same = row_ids == col_ids
            head_kept, tail_kept = jnp.where(same, head, 0.0), jnp.where(same, tail, 0.0)
            head_across = jnp.sum(head_kept, axis=0, keepdims=True)
            tail_across = jnp.sum(tail_kept, axis=0, keepdims=True)
            head_down = jnp.sum(head_kept, axis=1, keepdims=True)
            tail_down = jnp.sum(tail_kept, axis=1, keepdims=True)
            parts[turn, 2 * pair] = source[second, first] * (head_across - tail_down)
            parts[turn, 2 * pair + 1] = jnp.where(
                row_ids > col_ids, head * (head_across - head_down), tail * (tail_across - tail_down)
            )

    def distribute(source, turn):
        @pl.when(on_diagonal)
        def _():
            if turn == 0:
                crossed(0).wait_recv()
            make_parts(source, turn)
            for step in (3, 2, 1):
                reduce_copy(turn, step).start()
            total = parts[turn, mine]
            for step in (1, 2, 3):
                remote(
                    parts.at[turn, 0],
                    arrived.at[turn, step - 1],
                    r_send.at[turn, step - 1],
                    r_recv.at[turn, step - 1],
                    peer(step)[1],
                ).wait_recv()
                total = total + arrived[turn, step - 1]
            gen[turn, 0, mine] = STEP_SIZE * total
            for step in (3, 2, 1):
                gather_copy(turn, 0, step).start()
            for number in range(len(row_targets) + len(col_targets)):
                serve_copy(turn, number).start()

        @pl.when(off_diagonal)
        def _():
            for kind in (0, 1):
                view = gen.at[turn, kind, mine]
                remote(view, view, b_send.at[turn, kind, 0], a_recv.at[turn, kind], row_source).wait_recv()
                for step in (3, 2, 1):
                    gather_copy(turn, kind, step).start()

        for step in (1, 2, 3):
            gather_wait(turn, 0, step)

    identity = jnp.where(
        lax.broadcasted_iota(jnp.int32, (2 * B, 2 * B), 0) == lax.broadcasted_iota(jnp.int32, (2 * B, 2 * B), 1),
        1.0,
        0.0,
    ).astype(F32)

    def rotation(turn, kind, pair, sign):
        across = gen[turn, kind, 2 * pair] * sign
        mixed = gen[turn, kind, 2 * pair + 1] * sign
        lower = jnp.where(row_ids > col_ids, mixed, 0.0)
        higher = jnp.where(row_ids < col_ids, mixed, 0.0)
        full[:B, :B] = lower - lower.T
        full[B:, B:] = higher - higher.T
        full[B:, :B] = across
        full[:B, B:] = -across.T
        once = full[...]
        halves = split(once)
        twice = product(halves, halves)
        rest = 0.5 * identity + once * (1.0 / 6.0) + twice * (1.0 / 24.0)
        return split(identity + once + product(split(twice), split(rest)))

    def rotations(turn):
        for pair in (0, 1):
            rows_high[pair], rows_low[pair] = rotation(turn, 0, pair, -1.0)

        @pl.when(off_diagonal)
        def _():
            for step in (1, 2, 3):
                gather_wait(turn, 1, step)

        @pl.when(on_diagonal)
        def _():
            gen[turn, 1] = gen[turn, 0]

        for pair in (0, 1):
            cols_high[pair], cols_low[pair] = rotation(turn, 1, pair, 1.0)

    distribute(quad, 0)
    rotations(0)

    @pl.when(off_diagonal)
    def _():
        crossed(0).wait_recv()

    crossed(1).wait_recv()

    for pair in (0, 1):
        moved = product(split(quad[:, pl.ds(pair * 2 * B, 2 * B)]), (cols_high[pair], cols_low[pair]))
        half_done[:, block(pair)] = moved[:, :B]
        half_done[:, block(pair + 2)] = moved[:, B:]
    for pair in (0, 1):
        moved = product((rows_high[pair], rows_low[pair]), split(half_done[pl.ds(pair * 2 * B, 2 * B), :]))
        turned[block(pair), :] = moved[:B]
        turned[block(pair + 2), :] = moved[B:]

    distribute(turned, 1)
    rotations(1)

    def give_back(part, step):
        place, device = peer(step)
        return remote(
            done.at[place, block(part)],
            landed.at[mine, block(part)],
            z_send.at[part, step - 1],
            z_recv.at[part, step - 1],
            device,
        )

    half = pl.ds(pl.multiple_of(upper * B, B), B)
    for part in (0, 1):
        moved = product(
            (rows_high[part, half], rows_low[part, half]), split(turned[pl.ds(part * 2 * B, 2 * B), :])
        )
        for pair in (0, 1):
            final = product(split(moved[:, pair * 2 * B : (pair + 1) * 2 * B]), (cols_high[pair], cols_low[pair]))
            done[pair, block(part)] = final[:, :B]
            done[pair + 2, block(part)] = final[:, B:]
        for step in (3, 2, 1):
            give_back(part, step).start()
    out_ref[mine] = done[mine]
    for part in (0, 1):
        for step in (1, 2, 3):
            place = sender(step)
            remote(
                done.at[0, block(part)],
                landed.at[place, block(part)],
                z_send.at[part, step - 1],
                z_recv.at[part, step - 1],
                peer(step)[1],
            ).wait_recv()
    for step in (1, 2, 3):
        out_ref[sender(step)] = landed[sender(step)]

    for step in (1, 2, 3):
        share(step).wait_send()
    for part in (0, 1):
        cross(part).wait_send()
        for step in (1, 2, 3):
            give_back(part, step).wait_send()
    for turn in (0, 1):
        for step in (1, 2, 3):
            gather_copy(turn, 0, step).wait_send()

        @pl.when(on_diagonal)
        def _():
            for step in (1, 2, 3):
                reduce_copy(turn, step).wait_send()
            for number in range(len(row_targets) + len(col_targets)):
                serve_copy(turn, number).wait_send()

        @pl.when(off_diagonal)
        def _():
            for step in (1, 2, 3):
                gather_copy(turn, 1, step).wait_send()


def local(n_row, n_col, positions):
    dma = pltpu.SemaphoreType.DMA
    n_serve = n_col // 4 - 1 + n_row // 2 - 1
    return pl.pallas_call(
        functools.partial(kernel, n_row, n_col),
        out_shape=jax.ShapeDtypeStruct(positions.shape, F32),
        in_specs=[pl.BlockSpec(memory_space=pltpu.VMEM)],
        out_specs=pl.BlockSpec(memory_space=pltpu.VMEM),
        scratch_shapes=[
            pltpu.VMEM((4 * B, 4 * B), F32),
            pltpu.VMEM((4 * B, 4 * B), F32),
            pltpu.VMEM((4 * B, 4 * B), F32),
            pltpu.VMEM((2, 4, B, B), F32),
            pltpu.VMEM((2, 3, B, B), F32),
            pltpu.VMEM((2, 2, 4, B, B), F32),
            pltpu.VMEM((2 * B, 2 * B), F32),
            pltpu.VMEM((2, 2 * B, 2 * B), BF16),
            pltpu.VMEM((2, 2 * B, 2 * B), BF16),
            pltpu.VMEM((2, 2 * B, 2 * B), BF16),
            pltpu.VMEM((2, 2 * B, 2 * B), BF16),
            pltpu.VMEM((4, 2 * B, B), F32),
            pltpu.VMEM((4, 2 * B, B), F32),
            dma,
            dma((3,)),
            dma((3,)),
            dma((2,)),
            dma((2,)),
            dma((2, 3)),
            dma((2, 3)),
            dma((2, n_serve)),
            dma((2, 2)),
            dma((2, 2, 3)),
            dma((2, 2, 3)),
            dma((2, 3)),
            dma((2, 3)),
        ],
        compiler_params=pltpu.CompilerParams(collective_id=0, has_side_effects=True, vmem_limit_bytes=48 * 2**20),
    )(positions)


def solution(mesh):
    body = functools.partial(local, mesh.shape["row"], mesh.shape["col"])
    spec = P(None, "row", "col")
    return jax.shard_map(body, mesh=mesh, in_specs=(spec,), out_specs=spec, check_vma=False)
```

```python
import functools

import jax
import jax.numpy as jnp
from jax import lax
from jax.experimental import pallas as pl
from jax.experimental.pallas import tpu as pltpu
from jax.sharding import PartitionSpec as P

STEP_SIZE = 0.4
B = 128
MESH = pl.DeviceIdType.MESH
F32 = jnp.float32
BF16 = jnp.bfloat16
REACH = {1: (0,), 2: (0, 1), 4: (2, 1, -1, 0)}


def split(value):
    high = value.astype(BF16)
    return high, (value - high.astype(F32)).astype(BF16)


def product(left, right):
    dot = functools.partial(jnp.dot, preferred_element_type=F32)
    return dot(left[0], right[0]) + (dot(left[0], right[1]) + dot(left[1], right[0]))


def block(index):
    return pl.ds(index * B, B)


def kernel(
    n_row,
    n_col,
    source_ref,
    out_ref,
    pos_ref,
    quad,
    half_done,
    turned,
    parts,
    arrived,
    gen,
    full,
    rows_high,
    rows_low,
    cols_high,
    cols_low,
    done,
    landed,
    turn_rows,
    tri_out,
    tri_in,
    centre_out,
    centre_in,
    load_sem,
    keep_sem,
    ready,
    swap_send,
    swap_recv,
    raw_send,
    raw_recv,
    piece_send,
    piece_recv,
    p_send,
    p_recv,
    y_send,
    y_recv,
    r_send,
    r_recv,
    a_send,
    a_recv,
    b_send,
    b_recv,
    z_send,
    z_recv,
):
    n_quad = n_col // 4
    row = lax.axis_index("row")
    col = lax.axis_index("col")
    row_quad, upper = lax.rem(row, n_quad), lax.div(row, n_quad)
    col_high, low = lax.div(col, n_col // 2), lax.rem(col, 2)
    col_quad = lax.div(lax.rem(col, n_col // 2), 2)
    mine = 2 * col_high + low
    on_diagonal = row_quad == col_quad
    off_diagonal = row_quad != col_quad
    owner = jnp.logical_and(on_diagonal, upper == col_high)
    guest = jnp.logical_and(on_diagonal, upper != col_high)
    first_owner = jnp.logical_and(owner, low == 0)
    second_owner = jnp.logical_and(owner, low == 1)
    far_row = lax.rem(row + n_quad, n_row)

    def column(quad_id, place):
        return (n_col // 2) * lax.div(place, 2) + 2 * quad_id + lax.rem(place, 2)

    def peer(step):
        place = lax.rem(mine + step, 4)
        return place, (row, column(col_quad, place))

    def sender(step):
        return lax.rem(mine + 4 - step, 4)

    def remote(src, dst, send, recv, device):
        return pltpu.make_async_remote_copy(
            src_ref=src, dst_ref=dst, send_sem=send, recv_sem=recv, device_id=device, device_id_type=MESH
        )

    reach = REACH[n_row // 4]
    hops = sorted(range(1, n_quad), key=lambda hop: abs(hop % 4 - 2))
    row_targets = [(row, column(lax.rem(row_quad + hop, n_quad), mine)) for hop in hops]
    chip, core = lax.div(row, 2), lax.rem(row, 2)
    col_targets = []
    for hop in reach:
        there = lax.rem(chip + n_row // 2 + hop, n_row // 2)
        col_targets.append((2 * there + 1 - core, col))
        if hop != 0:
            col_targets.append((2 * there + core, col))
    row_source = (row, column(row_quad, mine))
    away = lax.rem(chip + n_row // 2 - lax.div(col_quad, 2), n_row // 2)
    wraps = lax.div(away + n_row // 8 - (1 if n_row >= 16 else 0), n_row // 4) if n_row >= 16 else lax.div(away, n_row // 4)
    col_source = (lax.rem(col_quad + n_quad * lax.rem(wraps, 2), n_row), col)

    load = pltpu.make_async_copy(source_ref, pos_ref, load_sem)
    load.start()

    barrier = pltpu.get_barrier_semaphore()

    def greet(device):
        pl.semaphore_signal(barrier, inc=1, device_id=device, device_id_type=MESH)

    @pl.when(on_diagonal)
    def _():
        for side in (0, 1):
            greet((far_row, column(col_quad, 2 * (1 - upper) + side)))

    for step in (1, 2, 3):
        greet((row, column(col_quad, sender(step))))

    @pl.when(off_diagonal)
    def _():
        greet((far_row, col))
        pl.semaphore_wait(barrier, 3 + 1 + 2)
        for device in (row_source, col_source):
            pl.semaphore_signal(ready, inc=1, device_id=device, device_id_type=MESH)

    @pl.when(on_diagonal)
    def _():
        for device in row_targets + col_targets:
            greet(device)

    @pl.when(owner)
    def _():
        pl.semaphore_wait(barrier, 3 + 4)

    @pl.when(guest)
    def _():
        pl.semaphore_wait(barrier, 3)

    load.wait()

    own_rows = pl.ds(pl.multiple_of(upper * 2 * B, 2 * B), 2 * B)
    far_rows = pl.ds(pl.multiple_of((1 - upper) * 2 * B, 2 * B), 2 * B)

    def lanes(place):
        return pl.ds(pl.multiple_of(place * B, B), B)

    def share(step):
        place, device = peer(step)
        return remote(
            pos_ref.at[place], quad.at[own_rows, lanes(mine)], p_send.at[step - 1], p_recv.at[step - 1], device
        )

    def raw(place):
        return remote(
            pos_ref.at[place],
            quad.at[own_rows, lanes(mine)],
            raw_send.at[place],
            raw_recv.at[low],
            (far_row, column(col_quad, place)),
        )

    row_ids = lax.broadcasted_iota(jnp.int32, (B, B), 0)
    col_ids = lax.broadcasted_iota(jnp.int32, (B, B), 1)

    def reduce_copy(turn, step):
        place, device = peer(step)
        return remote(
            parts.at[turn, place],
            arrived.at[turn, step - 1],
            r_send.at[turn, step - 1],
            r_recv.at[turn, step - 1],
            device,
        )

    def serve_copy(turn, number):
        if number < len(row_targets):
            kind, device = 0, row_targets[number]
        else:
            kind, device = 1, col_targets[number - len(row_targets)]
        return remote(
            gen.at[turn, 0, mine], gen.at[turn, kind, mine], a_send.at[turn, number], a_recv.at[turn, kind], device
        )

    def gather_copy(turn, kind, step):
        _, device = peer(step)
        return remote(
            gen.at[turn, kind, mine],
            gen.at[turn, kind, mine],
            b_send.at[turn, kind, step - 1],
            b_recv.at[turn, kind, step - 1],
            device,
        )

    def gather_wait(turn, kind, step):
        place = sender(step)
        _, device = peer(step)
        remote(
            gen.at[turn, kind, place],
            gen.at[turn, kind, place],
            b_send.at[turn, kind, step - 1],
            b_recv.at[turn, kind, step - 1],
            device,
        ).wait_recv()

    def centre(tile):
        kept = jnp.where(row_ids == col_ids, tile, 0.0)
        return jnp.sum(kept, axis=0, keepdims=True), jnp.sum(kept, axis=1, keepdims=True)

    partner = (row, column(col_quad, mine + 1 - 2 * low))
    here = gen.at[0, 0, mine]
    piece = remote(here, here, piece_send, piece_recv, (far_row, col))
    give_tri = remote(tri_out, tri_in, swap_send, swap_recv, partner)
    give_centre = remote(centre_out, centre_in, swap_send, swap_recv, partner)

    @pl.when(second_owner)
    def _():
        total = jnp.zeros((B, B), F32)
        for matrix in range(4):
            tile = pos_ref[matrix, B:]
            across, down = centre(tile)
            centre_out[matrix : matrix + 1] = across
            total = total + tile * (across - down)
        give_centre.start()
        tri_out[...] = total

    @pl.when(first_owner)
    def _():
        total = jnp.zeros((B, B), F32)
        for matrix in range(4):
            tile = pos_ref[matrix, :B]
            across, down = centre(tile)
            centre_out[matrix : matrix + 1] = across
            total = total + tile * (across - down)
        tri_out[...] = total
        give_tri.start()

    @pl.when(owner)
    def _():
        raw(0).start()
        raw(1).start()

    for step in (3, 2, 1):
        share(step).start()
    keep = pltpu.make_async_copy(pos_ref.at[mine], quad.at[own_rows, lanes(mine)], keep_sem)
    keep.start()

    @pl.when(second_owner)
    def _():
        give_tri.wait_recv()
        gen[0, 0, mine] = STEP_SIZE * jnp.where(row_ids > col_ids, tri_in[...], tri_out[...])

    @pl.when(first_owner)
    def _():
        give_centre.wait_recv()
        total = jnp.zeros((B, B), F32)
        for matrix in range(4):
            _, down = centre(jnp.broadcast_to(centre_in[matrix : matrix + 1], (B, B)))
            total = total + pos_ref[matrix, B:] * (centre_out[matrix : matrix + 1] - down)
        gen[0, 0, mine] = STEP_SIZE * total

    @pl.when(owner)
    def _():
        piece.start()
        raw(2).start()
        raw(3).start()

    def serve(turn):
        for number in range(len(row_targets) + len(col_targets)):
            serve_copy(turn, number).start()

    def pass_on(turn):
        for kind in (0, 1):
            view = gen.at[turn, kind, mine]
            remote(view, view, b_send.at[turn, kind, 0], a_recv.at[turn, kind], row_source).wait_recv()
            for step in (3, 2, 1):
                gather_copy(turn, kind, step).start()

    @pl.when(guest)
    def _():
        piece.wait_recv()

    @pl.when(on_diagonal)
    def _():
        for step in (3, 2, 1):
            gather_copy(0, 0, step).start()
        pl.semaphore_wait(ready, len(row_targets) + len(col_targets))
        serve(0)

    own_slab, far_slab = quad.at[own_rows], quad.at[far_rows]
    cross = remote(own_slab, own_slab, y_send, y_recv, (far_row, col))

    for step in (1, 2, 3):
        remote(
            pos_ref.at[0],
            quad.at[own_rows, lanes(sender(step))],
            p_send.at[step - 1],
            p_recv.at[step - 1],
            peer(step)[1],
        ).wait_recv()
    keep.wait()

    @pl.when(off_diagonal)
    def _():
        pass_on(0)
        cross.start()

    def span(side, number):
        return pl.ds(pl.multiple_of((2 * side + number) * B, B), B)

    @pl.when(on_diagonal)
    def _():
        for far in (0, 1):
            for near in (0, 1):
                there, back = span(1 - upper, far), span(upper, near)
                quad[there, back] = quad[back, there].T

    def make_parts(source, turn):
        for pair in (0, 1):
            first, second = block(2 * pair), block(2 * pair + 1)
            head, tail = source[first, first], source[second, second]
            same = row_ids == col_ids
            head_kept, tail_kept = jnp.where(same, head, 0.0), jnp.where(same, tail, 0.0)
            head_across = jnp.sum(head_kept, axis=0, keepdims=True)
            tail_across = jnp.sum(tail_kept, axis=0, keepdims=True)
            head_down = jnp.sum(head_kept, axis=1, keepdims=True)
            tail_down = jnp.sum(tail_kept, axis=1, keepdims=True)
            parts[turn, 2 * pair] = source[second, first] * (head_across - tail_down)
            parts[turn, 2 * pair + 1] = jnp.where(
                row_ids > col_ids, head * (head_across - head_down), tail * (tail_across - tail_down)
            )

    def distribute(source, turn):
        @pl.when(on_diagonal)
        def _():
            make_parts(source, turn)
            for step in (3, 2, 1):
                reduce_copy(turn, step).start()
            total = parts[turn, mine]
            for step in (1, 2, 3):
                remote(
                    parts.at[turn, 0],
                    arrived.at[turn, step - 1],
                    r_send.at[turn, step - 1],
                    r_recv.at[turn, step - 1],
                    peer(step)[1],
                ).wait_recv()
                total = total + arrived[turn, step - 1]
            gen[turn, 0, mine] = STEP_SIZE * total
            for step in (3, 2, 1):
                gather_copy(turn, 0, step).start()
            serve(turn)

    identity = jnp.where(
        lax.broadcasted_iota(jnp.int32, (2 * B, 2 * B), 0) == lax.broadcasted_iota(jnp.int32, (2 * B, 2 * B), 1),
        1.0,
        0.0,
    ).astype(F32)

    def rotation(turn, kind, pair, sign):
        whole = full.at[pair]
        across = gen[turn, kind, 2 * pair] * sign
        mixed = gen[turn, kind, 2 * pair + 1] * sign
        lower = jnp.where(row_ids > col_ids, mixed, 0.0)
        higher = jnp.where(row_ids < col_ids, mixed, 0.0)
        whole[:B, :B] = lower - lower.T
        whole[B:, B:] = higher - higher.T
        whole[B:, :B] = across
        whole[:B, B:] = -across.T
        once = whole[...]
        halves = split(once)
        twice = product(halves, halves)
        rest = 0.5 * identity + once * (1.0 / 6.0) + twice * (1.0 / 24.0)
        return identity + once + product(split(twice), split(rest))

    def rotations(turn):
        for step in (1, 2, 3):
            gather_wait(turn, 0, step)
        for pair in (0, 1):
            turn_rows[pair] = rotation(turn, 0, pair, -1.0)
        for pair in (0, 1):
            rows_high[pair], rows_low[pair] = split(turn_rows[pair])

        @pl.when(on_diagonal)
        def _():
            for pair in (0, 1):
                cols_high[pair], cols_low[pair] = split(turn_rows[pair].T)

        @pl.when(off_diagonal)
        def _():
            for step in (1, 2, 3):
                gather_wait(turn, 1, step)
            for pair in (0, 1):
                cols_high[pair], cols_low[pair] = split(rotation(turn, 1, pair, 1.0))

    rotations(0)

    @pl.when(on_diagonal)
    def _():
        for side in (0, 1):
            remote(
                pos_ref.at[0],
                quad.at[far_rows, lanes(2 * (1 - upper) + side)],
                raw_send.at[side],
                raw_recv.at[side],
                (far_row, col),
            ).wait_recv()

    @pl.when(off_diagonal)
    def _():
        pass_on(1)
        remote(far_slab, far_slab, y_send, y_recv, (far_row, col)).wait_recv()

    for pair in (0, 1):
        moved = product(split(quad[:, pl.ds(pair * 2 * B, 2 * B)]), (cols_high[pair], cols_low[pair]))
        half_done[:, block(pair)] = moved[:, :B]
        half_done[:, block(pair + 2)] = moved[:, B:]
    for pair in (0, 1):
        moved = product((rows_high[pair], rows_low[pair]), split(half_done[pl.ds(pair * 2 * B, 2 * B), :]))
        turned[block(pair), :] = moved[:B]
        turned[block(pair + 2), :] = moved[B:]

    distribute(turned, 1)
    rotations(1)

    def give_back(part, step):
        place, device = peer(step)
        return remote(
            done.at[place, block(part)],
            landed.at[mine, block(part)],
            z_send.at[part, step - 1],
            z_recv.at[part, step - 1],
            device,
        )

    half = pl.ds(pl.multiple_of(upper * B, B), B)
    for part in (0, 1):
        moved = product(
            (rows_high[part, half], rows_low[part, half]), split(turned[pl.ds(part * 2 * B, 2 * B), :])
        )
        for pair in (0, 1):
            final = product(split(moved[:, pair * 2 * B : (pair + 1) * 2 * B]), (cols_high[pair], cols_low[pair]))
            done[pair, block(part)] = final[:, :B]
            done[pair + 2, block(part)] = final[:, B:]
        for step in (3, 2, 1):
            give_back(part, step).start()
    out_ref[mine] = done[mine]
    for part in (0, 1):
        for step in (1, 2, 3):
            place = sender(step)
            remote(
                done.at[0, block(part)],
                landed.at[place, block(part)],
                z_send.at[part, step - 1],
                z_recv.at[part, step - 1],
                peer(step)[1],
            ).wait_recv()
    for step in (1, 2, 3):
        out_ref[sender(step)] = landed[sender(step)]

    for step in (1, 2, 3):
        share(step).wait_send()
    for part in (0, 1):
        for step in (1, 2, 3):
            give_back(part, step).wait_send()
    for turn in (0, 1):
        for step in (1, 2, 3):
            gather_copy(turn, 0, step).wait_send()

        @pl.when(on_diagonal)
        def _():
            if turn == 1:
                for step in (1, 2, 3):
                    reduce_copy(turn, step).wait_send()
            for number in range(len(row_targets) + len(col_targets)):
                serve_copy(turn, number).wait_send()

        @pl.when(off_diagonal)
        def _():
            for step in (1, 2, 3):
                gather_copy(turn, 1, step).wait_send()
            if turn == 0:
                cross.wait_send()

    @pl.when(first_owner)
    def _():
        give_tri.wait_send()

    @pl.when(second_owner)
    def _():
        give_centre.wait_send()

    @pl.when(owner)
    def _():
        piece.wait_send()
        for place in range(4):
            raw(place).wait_send()


def local(n_row, n_col, positions):
    dma = pltpu.SemaphoreType.DMA
    n_serve = n_col // 4 - 1 + n_row // 2 - 1
    return pl.pallas_call(
        functools.partial(kernel, n_row, n_col),
        out_shape=jax.ShapeDtypeStruct(positions.shape, F32),
        in_specs=[pl.BlockSpec(memory_space=pltpu.HBM)],
        out_specs=pl.BlockSpec(memory_space=pltpu.VMEM),
        scratch_shapes=[
            pltpu.VMEM((4, 2 * B, B), F32),
            pltpu.VMEM((4 * B, 4 * B), F32),
            pltpu.VMEM((4 * B, 4 * B), F32),
            pltpu.VMEM((4 * B, 4 * B), F32),
            pltpu.VMEM((2, 4, B, B), F32),
            pltpu.VMEM((2, 3, B, B), F32),
            pltpu.VMEM((2, 2, 4, B, B), F32),
            pltpu.VMEM((2, 2 * B, 2 * B), F32),
            pltpu.VMEM((2, 2 * B, 2 * B), BF16),
            pltpu.VMEM((2, 2 * B, 2 * B), BF16),
            pltpu.VMEM((2, 2 * B, 2 * B), BF16),
            pltpu.VMEM((2, 2 * B, 2 * B), BF16),
            pltpu.VMEM((4, 2 * B, B), F32),
            pltpu.VMEM((4, 2 * B, B), F32),
            pltpu.VMEM((2, 2 * B, 2 * B), F32),
            pltpu.VMEM((B, B), F32),
            pltpu.VMEM((B, B), F32),
            pltpu.VMEM((8, B), F32),
            pltpu.VMEM((8, B), F32),
            dma,
            dma,
            pltpu.SemaphoreType.REGULAR,
            dma,
            dma,
            dma((4,)),
            dma((2,)),
            dma,
            dma,
            dma((3,)),
            dma((3,)),
            dma,
            dma,
            dma((2, 3)),
            dma((2, 3)),
            dma((2, n_serve)),
            dma((2, 2)),
            dma((2, 2, 3)),
            dma((2, 2, 3)),
            dma((2, 3)),
            dma((2, 3)),
        ],
        compiler_params=pltpu.CompilerParams(collective_id=0, has_side_effects=True, vmem_limit_bytes=48 * 2**20),
    )(positions)


def solution(mesh):
    body = functools.partial(local, mesh.shape["row"], mesh.shape["col"])
    spec = P(None, "row", "col")
    return jax.shard_map(body, mesh=mesh, in_specs=(spec,), out_specs=spec, check_vma=False)
```

```python
import functools

import jax
import jax.numpy as jnp
from jax import lax
from jax.experimental import pallas as pl
from jax.experimental.pallas import tpu as pltpu
from jax.sharding import PartitionSpec as P

STEP_SIZE = 0.4
B = 128
MESH = pl.DeviceIdType.MESH
F32 = jnp.float32
BF16 = jnp.bfloat16
REACH = {1: (0,), 2: (0, 1), 4: (2, 1, -1, 0)}


def split(value):
    high = value.astype(BF16)
    return high, (value - high.astype(F32)).astype(BF16)


def product(left, right):
    dot = functools.partial(jnp.dot, preferred_element_type=F32)
    return dot(left[0], right[0]) + (dot(left[0], right[1]) + dot(left[1], right[0]))


def block(index):
    return pl.ds(index * B, B)


def kernel(
    n_row,
    n_col,
    source_ref,
    out_ref,
    pos_ref,
    quad,
    half_done,
    turned,
    parts,
    arrived,
    gen,
    full,
    rows_high,
    rows_low,
    cols_high,
    cols_low,
    done,
    landed,
    turn_rows,
    tri_out,
    tri_in,
    centre_out,
    centre_in,
    load_sem,
    keep_sem,
    ready,
    swap_send,
    swap_recv,
    raw_send,
    raw_recv,
    piece_send,
    piece_recv,
    f_send,
    f_recv,
    p_send,
    p_recv,
    y_send,
    y_recv,
    r_send,
    r_recv,
    a_send,
    a_recv,
    b_send,
    b_recv,
    z_send,
    z_recv,
):
    n_quad = n_col // 4
    row = lax.axis_index("row")
    col = lax.axis_index("col")
    row_quad, upper = lax.rem(row, n_quad), lax.div(row, n_quad)
    col_high, low = lax.div(col, n_col // 2), lax.rem(col, 2)
    col_quad = lax.div(lax.rem(col, n_col // 2), 2)
    mine = 2 * col_high + low
    on_diagonal = row_quad == col_quad
    off_diagonal = row_quad != col_quad
    owner = jnp.logical_and(on_diagonal, upper == col_high)
    guest = jnp.logical_and(on_diagonal, upper != col_high)
    first_owner = jnp.logical_and(owner, low == 0)
    second_owner = jnp.logical_and(owner, low == 1)
    core = lax.rem(row, 2)
    sibling = (row + 1 - 2 * core, col)
    leader = jnp.logical_and(off_diagonal, core == lax.rem(col_quad, 2))
    follower = core != lax.rem(col_quad, 2)
    far_row = lax.rem(row + n_quad, n_row)

    def column(quad_id, place):
        return (n_col // 2) * lax.div(place, 2) + 2 * quad_id + lax.rem(place, 2)

    def peer(step):
        place = 2 * (1 - col_high if step >= 2 else col_high) + (1 - low if step % 2 else low)
        return place, (row, column(col_quad, place))

    def sender(step):
        return peer(step)[0]

    def remote(src, dst, send, recv, device):
        return pltpu.make_async_remote_copy(
            src_ref=src, dst_ref=dst, send_sem=send, recv_sem=recv, device_id=device, device_id_type=MESH
        )

    reach = REACH[n_row // 4]
    hops = sorted(range(1, n_quad), key=lambda hop: abs(hop % 4 - 2))
    row_targets = [(row, column(lax.rem(row_quad + hop, n_quad), mine)) for hop in hops]
    chip = lax.div(row, 2)
    n_chip = n_row // 2

    def above(hop):
        return 2 * lax.rem(chip + n_chip + hop, n_chip) + core, col

    col_targets = [above(hop) for hop in reach if hop != 0]
    other_targets = [above(n_chip // 2 + hop) for hop in reach if hop != 0]
    row_source = (row, column(row_quad, mine))
    away = lax.rem(chip + n_row // 2 - lax.div(col_quad, 2), n_row // 2)
    wraps = lax.div(away + n_row // 8 - (1 if n_row >= 16 else 0), n_row // 4) if n_row >= 16 else lax.div(away, n_row // 4)
    col_source = (lax.rem(col_quad + n_quad * lax.rem(wraps, 2), n_row), col)
    col_owner = (col_quad + n_quad * col_high, col)
    near_owner = jnp.logical_and(leader, lax.rem(wraps, 2) == col_high)
    far_owner = jnp.logical_and(leader, lax.rem(wraps, 2) != col_high)

    load = pltpu.make_async_copy(source_ref, pos_ref, load_sem)
    load.start()

    barrier = pltpu.get_barrier_semaphore()

    def greet(device):
        pl.semaphore_signal(barrier, inc=1, device_id=device, device_id_type=MESH)

    @pl.when(on_diagonal)
    def _():
        for side in (0, 1):
            greet((far_row, column(col_quad, 2 * (1 - upper) + side)))

    for step in (1, 2, 3):
        greet((row, column(col_quad, sender(step))))

    @pl.when(off_diagonal)
    def _():
        greet((far_row, col))

    @pl.when(follower)
    def _():
        greet(sibling)

    @pl.when(on_diagonal)
    def _():
        for device in row_targets + col_targets:
            greet(device)

    @pl.when(owner)
    def _():
        for device in other_targets:
            greet(device)

    def answer(device):
        pl.semaphore_signal(ready, inc=1, device_id=device, device_id_type=MESH)

    @pl.when(follower)
    def _():
        pl.semaphore_wait(barrier, 3 + 1 + 1)
        answer(row_source)

    @pl.when(near_owner)
    def _():
        pl.semaphore_wait(barrier, 3 + 1 + 2 + 1)
        answer(row_source)
        answer(col_source)

    @pl.when(far_owner)
    def _():
        pl.semaphore_wait(barrier, 3 + 1 + 3 + 1)
        answer(row_source)
        answer(col_source)
        answer(col_owner)

    @pl.when(owner)
    def _():
        pl.semaphore_wait(barrier, 3 + 4 + 1)

    @pl.when(guest)
    def _():
        pl.semaphore_wait(barrier, 3 + 1)

    load.wait()

    own_rows = pl.ds(pl.multiple_of(upper * 2 * B, 2 * B), 2 * B)
    far_rows = pl.ds(pl.multiple_of((1 - upper) * 2 * B, 2 * B), 2 * B)

    def lanes(place):
        return pl.ds(pl.multiple_of(place * B, B), B)

    def share(step):
        place, device = peer(step)
        return remote(
            pos_ref.at[place], quad.at[own_rows, lanes(mine)], p_send.at[step - 1], p_recv.at[step - 1], device
        )

    def raw(place):
        return remote(
            pos_ref.at[place],
            quad.at[own_rows, lanes(mine)],
            raw_send.at[place],
            raw_recv.at[low],
            (far_row, column(col_quad, place)),
        )

    row_ids = lax.broadcasted_iota(jnp.int32, (B, B), 0)
    col_ids = lax.broadcasted_iota(jnp.int32, (B, B), 1)

    def reduce_copy(turn, step):
        place, device = peer(step)
        return remote(
            parts.at[turn, place],
            arrived.at[turn, step - 1],
            r_send.at[turn, step - 1],
            r_recv.at[turn, step - 1],
            device,
        )

    def serve_copy(turn, kind, number):
        device = (row_targets if kind == 0 else col_targets + other_targets)[number]
        slot = number + kind * len(row_targets)
        return remote(
            gen.at[turn, 0, mine], gen.at[turn, kind, mine], a_send.at[turn, slot], a_recv.at[turn, kind], device
        )

    def gather_copy(turn, kind, step):
        _, device = peer(step)
        return remote(
            gen.at[turn, kind, mine],
            gen.at[turn, kind, mine],
            b_send.at[turn, kind, step - 1],
            b_recv.at[turn, kind, step - 1],
            device,
        )

    def gather_wait(turn, kind, step):
        place = sender(step)
        _, device = peer(step)
        remote(
            gen.at[turn, kind, place],
            gen.at[turn, kind, place],
            b_send.at[turn, kind, step - 1],
            b_recv.at[turn, kind, step - 1],
            device,
        ).wait_recv()

    def centre(tile):
        kept = jnp.where(row_ids == col_ids, tile, 0.0)
        return jnp.sum(kept, axis=0, keepdims=True), jnp.sum(kept, axis=1, keepdims=True)

    partner = (row, column(col_quad, mine + 1 - 2 * low))
    here = gen.at[0, 0, mine]
    piece = remote(here, here, piece_send, piece_recv, (far_row, col))
    give_tri = remote(tri_out, tri_in, swap_send, swap_recv, partner)
    give_centre = remote(centre_out, centre_in, swap_send, swap_recv, partner)

    @pl.when(second_owner)
    def _():
        total = jnp.zeros((B, B), F32)
        for matrix in range(4):
            tile = pos_ref[matrix, B:]
            across, down = centre(tile)
            centre_out[matrix : matrix + 1] = across
            total = total + tile * (across - down)
        give_centre.start()
        tri_out[...] = total

    @pl.when(first_owner)
    def _():
        total = jnp.zeros((B, B), F32)
        for matrix in range(4):
            tile = pos_ref[matrix, :B]
            across, down = centre(tile)
            centre_out[matrix : matrix + 1] = across
            total = total + tile * (across - down)
        tri_out[...] = total
        give_tri.start()

    @pl.when(owner)
    def _():
        for place in range(4):
            raw(place).start()

    for step in (3, 2, 1):
        share(step).start()
    keep = pltpu.make_async_copy(pos_ref.at[mine], quad.at[own_rows, lanes(mine)], keep_sem)
    keep.start()

    @pl.when(second_owner)
    def _():
        give_tri.wait_recv()
        gen[0, 0, mine] = STEP_SIZE * jnp.where(row_ids > col_ids, tri_in[...], tri_out[...])

    @pl.when(first_owner)
    def _():
        give_centre.wait_recv()
        total = jnp.zeros((B, B), F32)
        for matrix in range(4):
            _, down = centre(jnp.broadcast_to(centre_in[matrix : matrix + 1], (B, B)))
            total = total + pos_ref[matrix, B:] * (centre_out[matrix : matrix + 1] - down)
        gen[0, 0, mine] = STEP_SIZE * total

    @pl.when(owner)
    def _():
        piece.start()
        pl.semaphore_wait(ready, len(row_targets) + len(col_targets) + len(other_targets))
        for number in reversed(range(len(col_targets) + len(other_targets))):
            serve_copy(0, 1, number).start()

    def serve_rows(turn):
        for number in range(len(row_targets)):
            serve_copy(turn, 0, number).start()

    def arrive(turn, kind):
        view = gen.at[turn, kind, mine]
        remote(view, view, b_send.at[turn, kind, 0], a_recv.at[turn, kind], row_source).wait_recv()
        for step in (3, 2, 1):
            gather_copy(turn, kind, step).start()

    def hand(turn, step, kind):
        place = mine if step == 0 else sender(step)
        return remote(
            gen.at[turn, kind, place], gen.at[turn, 1, place], f_send.at[turn, step], f_recv.at[turn, step], sibling
        )

    def pass_on_column(turn):
        @pl.when(leader)
        def _():
            arrive(turn, 1)
            hand(turn, 0, 1).start()

    @pl.when(guest)
    def _():
        piece.wait_recv()

    @pl.when(on_diagonal)
    def _():
        for step in (3, 2, 1):
            gather_copy(0, 0, step).start()

    @pl.when(guest)
    def _():
        pl.semaphore_wait(ready, len(row_targets) + len(col_targets))

    @pl.when(on_diagonal)
    def _():
        serve_rows(0)

    def cross(step):
        place = mine if step == 0 else sender(step)
        view = quad.at[own_rows, lanes(place)]
        return remote(pos_ref.at[mine] if step == 0 else view, view, y_send.at[step], y_recv.at[step], (far_row, col))

    def crossed(step):
        view = quad.at[far_rows, lanes(mine if step == 0 else sender(step))]
        return remote(view, view, y_send.at[step], y_recv.at[step], (far_row, col))

    def shared(step):
        view = quad.at[own_rows, lanes(sender(step))]
        return remote(pos_ref.at[0], view, p_send.at[step - 1], p_recv.at[step - 1], peer(step)[1])

    @pl.when(off_diagonal)
    def _():
        for step in (1, 2, 3):
            shared(step).wait_recv()

    @pl.when(on_diagonal)
    def _():
        for step in (1, 2, 3):
            shared(step).wait_recv()

    keep.wait()

    pass_on_column(0)

    @pl.when(follower)
    def _():
        hand(0, 0, 1).wait_recv()

    @pl.when(off_diagonal)
    def _():
        for step in range(4):
            cross(step).start()
        arrive(0, 0)

    def span(side, number):
        return pl.ds(pl.multiple_of((2 * side + number) * B, B), B)

    @pl.when(on_diagonal)
    def _():
        for far in (0, 1):
            for near in (0, 1):
                there, back = span(1 - upper, far), span(upper, near)
                quad[there, back] = quad[back, there].T

    def make_parts(source, turn):
        for pair in (0, 1):
            first, second = block(2 * pair), block(2 * pair + 1)
            head, tail = source[first, first], source[second, second]
            same = row_ids == col_ids
            head_kept, tail_kept = jnp.where(same, head, 0.0), jnp.where(same, tail, 0.0)
            head_across = jnp.sum(head_kept, axis=0, keepdims=True)
            tail_across = jnp.sum(tail_kept, axis=0, keepdims=True)
            head_down = jnp.sum(head_kept, axis=1, keepdims=True)
            tail_down = jnp.sum(tail_kept, axis=1, keepdims=True)
            parts[turn, 2 * pair] = source[second, first] * (head_across - tail_down)
            parts[turn, 2 * pair + 1] = jnp.where(
                row_ids > col_ids, head * (head_across - head_down), tail * (tail_across - tail_down)
            )

    def distribute(source, turn):
        @pl.when(on_diagonal)
        def _():
            make_parts(source, turn)
            for step in (3, 2, 1):
                reduce_copy(turn, step).start()
            total = parts[turn, mine]
            for step in (1, 2, 3):
                remote(
                    parts.at[turn, 0],
                    arrived.at[turn, step - 1],
                    r_send.at[turn, step - 1],
                    r_recv.at[turn, step - 1],
                    peer(step)[1],
                ).wait_recv()
                total = total + arrived[turn, step - 1]
            gen[turn, 0, mine] = STEP_SIZE * total
            for step in (3, 2, 1):
                gather_copy(turn, 0, step).start()
            for number in range(len(col_targets)):
                serve_copy(turn, 1, number).start()
            serve_rows(turn)

    identity = jnp.where(
        lax.broadcasted_iota(jnp.int32, (2 * B, 2 * B), 0) == lax.broadcasted_iota(jnp.int32, (2 * B, 2 * B), 1),
        1.0,
        0.0,
    ).astype(F32)

    def rotation(turn, kind, pair, sign):
        whole = full.at[pair]
        across = gen[turn, kind, 2 * pair] * sign
        mixed = gen[turn, kind, 2 * pair + 1] * sign
        lower = jnp.where(row_ids > col_ids, mixed, 0.0)
        higher = jnp.where(row_ids < col_ids, mixed, 0.0)
        whole[:B, :B] = lower - lower.T
        whole[B:, B:] = higher - higher.T
        whole[B:, :B] = across
        whole[:B, B:] = -across.T
        once = whole[...]
        halves = split(once)
        twice = product(halves, halves)
        rest = 0.5 * identity + once * (1.0 / 6.0) + twice * (1.0 / 24.0)
        return identity + once + product(split(twice), split(rest))

    def rotations(turn):
        for step in (1, 2, 3):
            gather_wait(turn, 0, step)

        @pl.when(on_diagonal)
        def _():
            for step in range(4):
                hand(turn, step, 0).start()

        @pl.when(leader)
        def _():
            for step in (1, 2, 3):
                gather_wait(turn, 1, step)
                hand(turn, step, 1).start()

        for pair in (0, 1):
            turn_rows[pair] = rotation(turn, 0, pair, -1.0)
        for pair in (0, 1):
            rows_high[pair], rows_low[pair] = split(turn_rows[pair])

        @pl.when(on_diagonal)
        def _():
            for pair in (0, 1):
                cols_high[pair], cols_low[pair] = split(turn_rows[pair].T)

        @pl.when(follower)
        def _():
            for step in range(1 if turn == 0 else 0, 4):
                hand(turn, step, 1).wait_recv()

        @pl.when(off_diagonal)
        def _():
            for pair in (0, 1):
                cols_high[pair], cols_low[pair] = split(rotation(turn, 1, pair, 1.0))

    rotations(0)

    @pl.when(on_diagonal)
    def _():
        for side in (0, 1):
            remote(
                pos_ref.at[0],
                quad.at[far_rows, lanes(2 * (1 - upper) + side)],
                raw_send.at[side],
                raw_recv.at[side],
                (far_row, col),
            ).wait_recv()

    @pl.when(off_diagonal)
    def _():
        arrive(1, 0)

    pass_on_column(1)

    @pl.when(off_diagonal)
    def _():
        for step in range(4):
            crossed(step).wait_recv()

    for pair in (0, 1):
        moved = product(split(quad[:, pl.ds(pair * 2 * B, 2 * B)]), (cols_high[pair], cols_low[pair]))
        half_done[:, block(pair)] = moved[:, :B]
        half_done[:, block(pair + 2)] = moved[:, B:]
    for pair in (0, 1):
        moved = product((rows_high[pair], rows_low[pair]), split(half_done[pl.ds(pair * 2 * B, 2 * B), :]))
        turned[block(pair), :] = moved[:B]
        turned[block(pair + 2), :] = moved[B:]

    distribute(turned, 1)
    rotations(1)

    def give_back(part, step):
        place, device = peer(step)
        return remote(
            done.at[place, block(part)],
            landed.at[mine, block(part)],
            z_send.at[part, step - 1],
            z_recv.at[part, step - 1],
            device,
        )

    half = pl.ds(pl.multiple_of(upper * B, B), B)
    for part in (0, 1):
        moved = product(
            (rows_high[part, half], rows_low[part, half]), split(turned[pl.ds(part * 2 * B, 2 * B), :])
        )
        for pair in (0, 1):
            final = product(split(moved[:, pair * 2 * B : (pair + 1) * 2 * B]), (cols_high[pair], cols_low[pair]))
            done[pair, block(part)] = final[:, :B]
            done[pair + 2, block(part)] = final[:, B:]
        for step in (3, 2, 1):
            give_back(part, step).start()
    out_ref[mine] = done[mine]
    for part in (0, 1):
        for step in (1, 2, 3):
            place = sender(step)
            remote(
                done.at[0, block(part)],
                landed.at[place, block(part)],
                z_send.at[part, step - 1],
                z_recv.at[part, step - 1],
                peer(step)[1],
            ).wait_recv()
    for step in (1, 2, 3):
        out_ref[sender(step)] = landed[sender(step)]

    for step in (1, 2, 3):
        share(step).wait_send()
    for part in (0, 1):
        for step in (1, 2, 3):
            give_back(part, step).wait_send()
    for turn in (0, 1):
        for step in (1, 2, 3):
            gather_copy(turn, 0, step).wait_send()

        @pl.when(on_diagonal)
        def _():
            if turn == 1:
                for step in (1, 2, 3):
                    reduce_copy(turn, step).wait_send()
                for number in range(len(col_targets)):
                    serve_copy(turn, 1, number).wait_send()
            for number in range(len(row_targets)):
                serve_copy(turn, 0, number).wait_send()

            for step in range(4):
                hand(turn, step, 0).wait_send()

        @pl.when(leader)
        def _():
            for step in (1, 2, 3):
                gather_copy(turn, 1, step).wait_send()
            for step in range(4):
                hand(turn, step, 1).wait_send()

        @pl.when(off_diagonal)
        def _():
            if turn == 0:
                for step in range(4):
                    cross(step).wait_send()

    @pl.when(first_owner)
    def _():
        give_tri.wait_send()

    @pl.when(second_owner)
    def _():
        give_centre.wait_send()

    @pl.when(owner)
    def _():
        piece.wait_send()
        for number in range(len(col_targets) + len(other_targets)):
            serve_copy(0, 1, number).wait_send()
        for place in range(4):
            raw(place).wait_send()


def local(n_row, n_col, positions):
    dma = pltpu.SemaphoreType.DMA
    n_serve = n_col // 4 - 1 + 2 * (n_row // 4 - 1)
    return pl.pallas_call(
        functools.partial(kernel, n_row, n_col),
        out_shape=jax.ShapeDtypeStruct(positions.shape, F32),
        in_specs=[pl.BlockSpec(memory_space=pltpu.HBM)],
        out_specs=pl.BlockSpec(memory_space=pltpu.VMEM),
        scratch_shapes=[
            pltpu.VMEM((4, 2 * B, B), F32),
            pltpu.VMEM((4 * B, 4 * B), F32),
            pltpu.VMEM((4 * B, 4 * B), F32),
            pltpu.VMEM((4 * B, 4 * B), F32),
            pltpu.VMEM((2, 4, B, B), F32),
            pltpu.VMEM((2, 3, B, B), F32),
            pltpu.VMEM((2, 2, 4, B, B), F32),
            pltpu.VMEM((2, 2 * B, 2 * B), F32),
            pltpu.VMEM((2, 2 * B, 2 * B), BF16),
            pltpu.VMEM((2, 2 * B, 2 * B), BF16),
            pltpu.VMEM((2, 2 * B, 2 * B), BF16),
            pltpu.VMEM((2, 2 * B, 2 * B), BF16),
            pltpu.VMEM((4, 2 * B, B), F32),
            pltpu.VMEM((4, 2 * B, B), F32),
            pltpu.VMEM((2, 2 * B, 2 * B), F32),
            pltpu.VMEM((B, B), F32),
            pltpu.VMEM((B, B), F32),
            pltpu.VMEM((8, B), F32),
            pltpu.VMEM((8, B), F32),
            dma,
            dma,
            pltpu.SemaphoreType.REGULAR,
            dma,
            dma,
            dma((4,)),
            dma((2,)),
            dma,
            dma,
            dma((2, 4)),
            dma((2, 4)),
            dma((3,)),
            dma((3,)),
            dma((4,)),
            dma((4,)),
            dma((2, 3)),
            dma((2, 3)),
            dma((2, n_serve)),
            dma((2, 2)),
            dma((2, 2, 3)),
            dma((2, 2, 3)),
            dma((2, 3)),
            dma((2, 3)),
        ],
        compiler_params=pltpu.CompilerParams(collective_id=0, has_side_effects=True, vmem_limit_bytes=48 * 2**20),
    )(positions)


def solution(mesh):
    body = functools.partial(local, mesh.shape["row"], mesh.shape["col"])
    spec = P(None, "row", "col")
    return jax.shard_map(body, mesh=mesh, in_specs=(spec,), out_specs=spec, check_vma=False)
```

```python
import functools

import jax
import jax.numpy as jnp
from jax import lax
from jax.experimental import pallas as pl
from jax.experimental.pallas import tpu as pltpu
from jax.sharding import PartitionSpec as P

STEP_SIZE = 0.4
B = 128
MESH = pl.DeviceIdType.MESH
F32 = jnp.float32
BF16 = jnp.bfloat16
REACH = {1: (0,), 2: (0, 1), 4: (2, 1, -1, 0)}


def split(value):
    high = value.astype(BF16)
    return high, (value - high.astype(F32)).astype(BF16)


def product(left, right):
    dot = functools.partial(jnp.dot, preferred_element_type=F32)
    return dot(left[0], right[0]) + (dot(left[0], right[1]) + dot(left[1], right[0]))


def block(index):
    return pl.ds(index * B, B)


def kernel(
    n_row,
    n_col,
    source_ref,
    out_ref,
    pos_ref,
    quad,
    half_done,
    turned,
    parts,
    arrived,
    gen,
    full,
    rows_high,
    rows_low,
    cols_high,
    cols_low,
    done,
    landed,
    turn_rows,
    tri_out,
    tri_in,
    centre_out,
    centre_in,
    load_sem,
    keep_sem,
    ready,
    swap_send,
    swap_recv,
    raw_send,
    raw_recv,
    piece_send,
    piece_recv,
    f_send,
    f_recv,
    p_send,
    p_recv,
    y_send,
    y_recv,
    r_send,
    r_recv,
    a_send,
    a_recv,
    b_send,
    b_recv,
    z_send,
    z_recv,
):
    n_quad = n_col // 4
    row = lax.axis_index("row")
    col = lax.axis_index("col")
    row_quad, upper = lax.rem(row, n_quad), lax.div(row, n_quad)
    col_high, low = lax.div(col, n_col // 2), lax.rem(col, 2)
    col_quad = lax.div(lax.rem(col, n_col // 2), 2)
    mine = 2 * col_high + low
    on_diagonal = row_quad == col_quad
    off_diagonal = row_quad != col_quad
    owner = jnp.logical_and(on_diagonal, upper == col_high)
    guest = jnp.logical_and(on_diagonal, upper != col_high)
    first_owner = jnp.logical_and(owner, low == 0)
    second_owner = jnp.logical_and(owner, low == 1)
    core = lax.rem(row, 2)
    sibling = (row + 1 - 2 * core, col)
    leader = jnp.logical_and(off_diagonal, core == lax.rem(col_quad, 2))
    follower = core != lax.rem(col_quad, 2)
    far_row = lax.rem(row + n_quad, n_row)

    def column(quad_id, place):
        return (n_col // 2) * lax.div(place, 2) + 2 * quad_id + lax.rem(place, 2)

    def peer(step):
        place = 2 * (1 - col_high if step >= 2 else col_high) + (1 - low if step % 2 else low)
        return place, (row, column(col_quad, place))

    def sender(step):
        return peer(step)[0]

    def remote(src, dst, send, recv, device):
        return pltpu.make_async_remote_copy(
            src_ref=src, dst_ref=dst, send_sem=send, recv_sem=recv, device_id=device, device_id_type=MESH
        )

    reach = REACH[n_row // 4]
    hops = sorted(range(1, n_quad), key=lambda hop: abs(hop % 4 - 2))
    row_targets = [(row, column(lax.rem(row_quad + hop, n_quad), mine)) for hop in hops]
    chip = lax.div(row, 2)
    n_chip = n_row // 2

    def above(hop):
        return 2 * lax.rem(chip + n_chip + hop, n_chip) + core, col

    col_targets = [above(hop) for hop in reach if hop != 0]
    other_targets = [above(n_chip // 2 + hop) for hop in reach if hop != 0]
    col_hops = [hop % n_chip for hop in reach if hop != 0] + [(n_chip // 2 + hop) % n_chip for hop in reach if hop != 0]
    far_first = sorted(range(len(col_hops)), key=lambda number: -min(col_hops[number], n_chip - col_hops[number]))
    row_source = (row, column(row_quad, mine))
    away = lax.rem(chip + n_row // 2 - lax.div(col_quad, 2), n_row // 2)
    wraps = lax.div(away + n_row // 8 - (1 if n_row >= 16 else 0), n_row // 4) if n_row >= 16 else lax.div(away, n_row // 4)
    col_source = (lax.rem(col_quad + n_quad * lax.rem(wraps, 2), n_row), col)
    col_owner = (col_quad + n_quad * col_high, col)
    near_owner = jnp.logical_and(leader, lax.rem(wraps, 2) == col_high)
    far_owner = jnp.logical_and(leader, lax.rem(wraps, 2) != col_high)

    load = pltpu.make_async_copy(source_ref, pos_ref, load_sem)
    load.start()

    barrier = pltpu.get_barrier_semaphore()

    def greet(device):
        pl.semaphore_signal(barrier, inc=1, device_id=device, device_id_type=MESH)

    @pl.when(on_diagonal)
    def _():
        for side in (0, 1):
            greet((far_row, column(col_quad, 2 * (1 - upper) + side)))

    for step in (1, 2, 3):
        greet((row, column(col_quad, sender(step))))

    @pl.when(off_diagonal)
    def _():
        greet((far_row, col))

    @pl.when(follower)
    def _():
        greet(sibling)

    @pl.when(on_diagonal)
    def _():
        for device in row_targets + col_targets:
            greet(device)

    @pl.when(owner)
    def _():
        for device in other_targets:
            greet(device)

    def answer(device):
        pl.semaphore_signal(ready, inc=1, device_id=device, device_id_type=MESH)

    @pl.when(follower)
    def _():
        pl.semaphore_wait(barrier, 3 + 1 + 1)
        answer(row_source)

    @pl.when(near_owner)
    def _():
        pl.semaphore_wait(barrier, 3 + 1 + 2 + 1)
        answer(row_source)
        answer(col_source)

    @pl.when(far_owner)
    def _():
        pl.semaphore_wait(barrier, 3 + 1 + 3 + 1)
        answer(row_source)
        answer(col_source)
        answer(col_owner)

    @pl.when(owner)
    def _():
        pl.semaphore_wait(barrier, 3 + 4 + 1)

    @pl.when(guest)
    def _():
        pl.semaphore_wait(barrier, 3 + 1)

    load.wait()

    own_rows = pl.ds(pl.multiple_of(upper * 2 * B, 2 * B), 2 * B)
    far_rows = pl.ds(pl.multiple_of((1 - upper) * 2 * B, 2 * B), 2 * B)

    def lanes(place):
        return pl.ds(pl.multiple_of(place * B, B), B)

    def share(step):
        place, device = peer(step)
        return remote(
            pos_ref.at[place], quad.at[own_rows, lanes(mine)], p_send.at[step - 1], p_recv.at[step - 1], device
        )

    def raw(place):
        return remote(
            pos_ref.at[place],
            quad.at[own_rows, lanes(mine)],
            raw_send.at[place],
            raw_recv.at[low],
            (far_row, column(col_quad, place)),
        )

    row_ids = lax.broadcasted_iota(jnp.int32, (B, B), 0)
    col_ids = lax.broadcasted_iota(jnp.int32, (B, B), 1)

    def reduce_copy(turn, step):
        place, device = peer(step)
        return remote(
            parts.at[turn, place],
            arrived.at[turn, step - 1],
            r_send.at[turn, step - 1],
            r_recv.at[turn, step - 1],
            device,
        )

    def serve_copy(turn, kind, number):
        device = (row_targets if kind == 0 else col_targets + other_targets)[number]
        slot = number + kind * len(row_targets)
        return remote(
            gen.at[turn, 0, mine], gen.at[turn, kind, mine], a_send.at[turn, slot], a_recv.at[turn, kind], device
        )

    def gather_copy(turn, kind, step):
        _, device = peer(step)
        return remote(
            gen.at[turn, kind, mine],
            gen.at[turn, kind, mine],
            b_send.at[turn, kind, step - 1],
            b_recv.at[turn, kind, step - 1],
            device,
        )

    def gather_wait(turn, kind, step):
        place = sender(step)
        _, device = peer(step)
        remote(
            gen.at[turn, kind, place],
            gen.at[turn, kind, place],
            b_send.at[turn, kind, step - 1],
            b_recv.at[turn, kind, step - 1],
            device,
        ).wait_recv()

    def centre(tile):
        kept = jnp.where(row_ids == col_ids, tile, 0.0)
        return jnp.sum(kept, axis=0, keepdims=True), jnp.sum(kept, axis=1, keepdims=True)

    partner = (row, column(col_quad, mine + 1 - 2 * low))
    here = gen.at[0, 0, mine]
    piece = remote(here, here, piece_send, piece_recv, (far_row, col))
    give_tri = remote(tri_out, tri_in, swap_send, swap_recv, partner)
    give_centre = remote(centre_out, centre_in, swap_send, swap_recv, partner)

    @pl.when(second_owner)
    def _():
        total = jnp.zeros((B, B), F32)
        for matrix in range(4):
            tile = pos_ref[matrix, B:]
            across, down = centre(tile)
            centre_out[matrix : matrix + 1] = across
            total = total + tile * (across - down)
        give_centre.start()
        tri_out[...] = total

    @pl.when(first_owner)
    def _():
        total = jnp.zeros((B, B), F32)
        for matrix in range(4):
            tile = pos_ref[matrix, :B]
            across, down = centre(tile)
            centre_out[matrix : matrix + 1] = across
            total = total + tile * (across - down)
        tri_out[...] = total
        give_tri.start()

    @pl.when(owner)
    def _():
        for place in range(3):
            raw(place).start()

    for step in (3, 2, 1):
        share(step).start()
    keep = pltpu.make_async_copy(pos_ref.at[mine], quad.at[own_rows, lanes(mine)], keep_sem)
    keep.start()

    @pl.when(second_owner)
    def _():
        give_tri.wait_recv()
        gen[0, 0, mine] = STEP_SIZE * jnp.where(row_ids > col_ids, tri_in[...], tri_out[...])

    @pl.when(first_owner)
    def _():
        give_centre.wait_recv()
        total = jnp.zeros((B, B), F32)
        for matrix in range(4):
            _, down = centre(jnp.broadcast_to(centre_in[matrix : matrix + 1], (B, B)))
            total = total + pos_ref[matrix, B:] * (centre_out[matrix : matrix + 1] - down)
        gen[0, 0, mine] = STEP_SIZE * total

    @pl.when(owner)
    def _():
        piece.start()
        raw(3).start()
        pl.semaphore_wait(ready, len(row_targets) + len(col_targets) + len(other_targets))
        for number in far_first:
            serve_copy(0, 1, number).start()

    def serve_rows(turn):
        for number in range(len(row_targets)):
            serve_copy(turn, 0, number).start()

    def arrive(turn, kind):
        view = gen.at[turn, kind, mine]
        remote(view, view, b_send.at[turn, kind, 0], a_recv.at[turn, kind], row_source).wait_recv()
        for step in (3, 2, 1):
            gather_copy(turn, kind, step).start()

    def hand(turn, step, kind):
        place = mine if step == 0 else sender(step)
        return remote(
            gen.at[turn, kind, place], gen.at[turn, 1, place], f_send.at[turn, step], f_recv.at[turn, step], sibling
        )

    def pass_on_column(turn):
        @pl.when(leader)
        def _():
            arrive(turn, 1)
            hand(turn, 0, 1).start()

    @pl.when(guest)
    def _():
        piece.wait_recv()

    @pl.when(on_diagonal)
    def _():
        for step in (3, 2, 1):
            gather_copy(0, 0, step).start()

    @pl.when(guest)
    def _():
        pl.semaphore_wait(ready, len(row_targets) + len(col_targets))

    @pl.when(on_diagonal)
    def _():
        serve_rows(0)

    @pl.when(owner)
    def _():
        for number in far_first:
            serve_copy(0, 1, number).wait_send()

    @pl.when(on_diagonal)
    def _():
        hand(0, 0, 0).start()

    def cross(step):
        place = mine if step == 0 else sender(step)
        view = quad.at[own_rows, lanes(place)]
        return remote(pos_ref.at[mine] if step == 0 else view, view, y_send.at[step], y_recv.at[step], (far_row, col))

    def crossed(step):
        view = quad.at[far_rows, lanes(mine if step == 0 else sender(step))]
        return remote(view, view, y_send.at[step], y_recv.at[step], (far_row, col))

    def shared(step):
        view = quad.at[own_rows, lanes(sender(step))]
        return remote(pos_ref.at[0], view, p_send.at[step - 1], p_recv.at[step - 1], peer(step)[1])

    @pl.when(off_diagonal)
    def _():
        for step in (1, 2, 3):
            shared(step).wait_recv()

    @pl.when(on_diagonal)
    def _():
        for step in (1, 2, 3):
            shared(step).wait_recv()

    keep.wait()

    pass_on_column(0)

    @pl.when(follower)
    def _():
        hand(0, 0, 1).wait_recv()

    @pl.when(off_diagonal)
    def _():
        for step in range(2):
            cross(step).start()
        arrive(0, 0)
        for step in range(2, 4):
            crossed(step - 2).wait_recv()
            cross(step).start()

    def span(side, number):
        return pl.ds(pl.multiple_of((2 * side + number) * B, B), B)

    @pl.when(on_diagonal)
    def _():
        for far in (0, 1):
            for near in (0, 1):
                there, back = span(1 - upper, far), span(upper, near)
                quad[there, back] = quad[back, there].T

    def make_parts(source, turn):
        for pair in (0, 1):
            first, second = block(2 * pair), block(2 * pair + 1)
            head, tail = source[first, first], source[second, second]
            same = row_ids == col_ids
            head_kept, tail_kept = jnp.where(same, head, 0.0), jnp.where(same, tail, 0.0)
            head_across = jnp.sum(head_kept, axis=0, keepdims=True)
            tail_across = jnp.sum(tail_kept, axis=0, keepdims=True)
            head_down = jnp.sum(head_kept, axis=1, keepdims=True)
            tail_down = jnp.sum(tail_kept, axis=1, keepdims=True)
            parts[turn, 2 * pair] = source[second, first] * (head_across - tail_down)
            parts[turn, 2 * pair + 1] = jnp.where(
                row_ids > col_ids, head * (head_across - head_down), tail * (tail_across - tail_down)
            )

    def distribute(source, turn):
        @pl.when(on_diagonal)
        def _():
            make_parts(source, turn)
            for step in (3, 2, 1):
                reduce_copy(turn, step).start()
            total = parts[turn, mine]
            for step in (1, 2, 3):
                remote(
                    parts.at[turn, 0],
                    arrived.at[turn, step - 1],
                    r_send.at[turn, step - 1],
                    r_recv.at[turn, step - 1],
                    peer(step)[1],
                ).wait_recv()
                total = total + arrived[turn, step - 1]
            gen[turn, 0, mine] = STEP_SIZE * total
            for number in range(len(col_targets)):
                serve_copy(turn, 1, number).start()
            serve_rows(turn)
            for step in (3, 2, 1):
                gather_copy(turn, 0, step).start()

    identity = jnp.where(
        lax.broadcasted_iota(jnp.int32, (2 * B, 2 * B), 0) == lax.broadcasted_iota(jnp.int32, (2 * B, 2 * B), 1),
        1.0,
        0.0,
    ).astype(F32)

    def rotation(turn, kind, pair, sign):
        whole = full.at[pair]
        across = gen[turn, kind, 2 * pair] * sign
        mixed = gen[turn, kind, 2 * pair + 1] * sign
        lower = jnp.where(row_ids > col_ids, mixed, 0.0)
        higher = jnp.where(row_ids < col_ids, mixed, 0.0)
        whole[:B, :B] = lower - lower.T
        whole[B:, B:] = higher - higher.T
        whole[B:, :B] = across
        whole[:B, B:] = -across.T
        once = whole[...]
        halves = split(once)
        twice = product(halves, halves)
        rest = 0.5 * identity + once * (1.0 / 6.0) + twice * (1.0 / 24.0)
        return identity + once + product(split(twice), split(rest))

    def rotations(turn):
        for step in (1, 2, 3):
            gather_wait(turn, 0, step)

        @pl.when(on_diagonal)
        def _():
            for step in range(1 if turn == 0 else 0, 4):
                hand(turn, step, 0).start()

        @pl.when(leader)
        def _():
            for step in (1, 2, 3):
                gather_wait(turn, 1, step)
                hand(turn, step, 1).start()

        for pair in (0, 1):
            turn_rows[pair] = rotation(turn, 0, pair, -1.0)
        for pair in (0, 1):
            rows_high[pair], rows_low[pair] = split(turn_rows[pair])

        @pl.when(on_diagonal)
        def _():
            for pair in (0, 1):
                cols_high[pair], cols_low[pair] = split(turn_rows[pair].T)

        @pl.when(follower)
        def _():
            for step in range(1 if turn == 0 else 0, 4):
                hand(turn, step, 1).wait_recv()

        @pl.when(off_diagonal)
        def _():
            for pair in (0, 1):
                cols_high[pair], cols_low[pair] = split(rotation(turn, 1, pair, 1.0))

    rotations(0)

    @pl.when(on_diagonal)
    def _():
        for side in (0, 1):
            remote(
                pos_ref.at[0],
                quad.at[far_rows, lanes(2 * (1 - upper) + side)],
                raw_send.at[side],
                raw_recv.at[side],
                (far_row, col),
            ).wait_recv()

    @pl.when(off_diagonal)
    def _():
        arrive(1, 0)

    pass_on_column(1)

    @pl.when(off_diagonal)
    def _():
        for step in range(2, 4):
            crossed(step).wait_recv()

    for pair in (0, 1):
        moved = product(split(quad[:, pl.ds(pair * 2 * B, 2 * B)]), (cols_high[pair], cols_low[pair]))
        half_done[:, block(pair)] = moved[:, :B]
        half_done[:, block(pair + 2)] = moved[:, B:]
    for pair in (0, 1):
        moved = product((rows_high[pair], rows_low[pair]), split(half_done[pl.ds(pair * 2 * B, 2 * B), :]))
        turned[block(pair), :] = moved[:B]
        turned[block(pair + 2), :] = moved[B:]

    distribute(turned, 1)
    rotations(1)

    def give_back(part, step):
        place, device = peer(step)
        return remote(
            done.at[place, block(part)],
            landed.at[mine, block(part)],
            z_send.at[part, step - 1],
            z_recv.at[part, step - 1],
            device,
        )

    half = pl.ds(pl.multiple_of(upper * B, B), B)
    for part in (0, 1):
        moved = product(
            (rows_high[part, half], rows_low[part, half]), split(turned[pl.ds(part * 2 * B, 2 * B), :])
        )
        for pair in (0, 1):
            final = product(split(moved[:, pair * 2 * B : (pair + 1) * 2 * B]), (cols_high[pair], cols_low[pair]))
            done[pair, block(part)] = final[:, :B]
            done[pair + 2, block(part)] = final[:, B:]
        for step in (3, 2, 1):
            give_back(part, step).start()
    out_ref[mine] = done[mine]
    for part in (0, 1):
        for step in (1, 2, 3):
            place = sender(step)
            remote(
                done.at[0, block(part)],
                landed.at[place, block(part)],
                z_send.at[part, step - 1],
                z_recv.at[part, step - 1],
                peer(step)[1],
            ).wait_recv()
    for step in (1, 2, 3):
        out_ref[sender(step)] = landed[sender(step)]

    for step in (1, 2, 3):
        share(step).wait_send()
    for part in (0, 1):
        for step in (1, 2, 3):
            give_back(part, step).wait_send()
    for turn in (0, 1):
        for step in (1, 2, 3):
            gather_copy(turn, 0, step).wait_send()

        @pl.when(on_diagonal)
        def _():
            if turn == 1:
                for step in (1, 2, 3):
                    reduce_copy(turn, step).wait_send()
                for number in range(len(col_targets)):
                    serve_copy(turn, 1, number).wait_send()
            for number in range(len(row_targets)):
                serve_copy(turn, 0, number).wait_send()

            for step in range(4):
                hand(turn, step, 0).wait_send()

        @pl.when(leader)
        def _():
            for step in (1, 2, 3):
                gather_copy(turn, 1, step).wait_send()
            for step in range(4):
                hand(turn, step, 1).wait_send()

        @pl.when(off_diagonal)
        def _():
            if turn == 0:
                for step in range(4):
                    cross(step).wait_send()

    @pl.when(first_owner)
    def _():
        give_tri.wait_send()

    @pl.when(second_owner)
    def _():
        give_centre.wait_send()

    @pl.when(owner)
    def _():
        piece.wait_send()
        for place in range(4):
            raw(place).wait_send()


def local(n_row, n_col, positions):
    dma = pltpu.SemaphoreType.DMA
    n_serve = n_col // 4 - 1 + 2 * (n_row // 4 - 1)
    return pl.pallas_call(
        functools.partial(kernel, n_row, n_col),
        out_shape=jax.ShapeDtypeStruct(positions.shape, F32),
        in_specs=[pl.BlockSpec(memory_space=pltpu.HBM)],
        out_specs=pl.BlockSpec(memory_space=pltpu.VMEM),
        scratch_shapes=[
            pltpu.VMEM((4, 2 * B, B), F32),
            pltpu.VMEM((4 * B, 4 * B), F32),
            pltpu.VMEM((4 * B, 4 * B), F32),
            pltpu.VMEM((4 * B, 4 * B), F32),
            pltpu.VMEM((2, 4, B, B), F32),
            pltpu.VMEM((2, 3, B, B), F32),
            pltpu.VMEM((2, 2, 4, B, B), F32),
            pltpu.VMEM((2, 2 * B, 2 * B), F32),
            pltpu.VMEM((2, 2 * B, 2 * B), BF16),
            pltpu.VMEM((2, 2 * B, 2 * B), BF16),
            pltpu.VMEM((2, 2 * B, 2 * B), BF16),
            pltpu.VMEM((2, 2 * B, 2 * B), BF16),
            pltpu.VMEM((4, 2 * B, B), F32),
            pltpu.VMEM((4, 2 * B, B), F32),
            pltpu.VMEM((2, 2 * B, 2 * B), F32),
            pltpu.VMEM((B, B), F32),
            pltpu.VMEM((B, B), F32),
            pltpu.VMEM((8, B), F32),
            pltpu.VMEM((8, B), F32),
            dma,
            dma,
            pltpu.SemaphoreType.REGULAR,
            dma,
            dma,
            dma((4,)),
            dma((2,)),
            dma,
            dma,
            dma((2, 4)),
            dma((2, 4)),
            dma((3,)),
            dma((3,)),
            dma((4,)),
            dma((4,)),
            dma((2, 3)),
            dma((2, 3)),
            dma((2, n_serve)),
            dma((2, 2)),
            dma((2, 2, 3)),
            dma((2, 2, 3)),
            dma((2, 3)),
            dma((2, 3)),
        ],
        compiler_params=pltpu.CompilerParams(collective_id=0, has_side_effects=True, vmem_limit_bytes=48 * 2**20),
    )(pltpu.with_memory_space_constraint(positions, pltpu.HBM))


def solution(mesh):
    body = functools.partial(local, mesh.shape["row"], mesh.shape["col"])
    spec = P(None, "row", "col")
    return jax.shard_map(body, mesh=mesh, in_specs=(spec,), out_specs=spec, check_vma=False)
```

```python
import functools

import jax
import jax.numpy as jnp
from jax import lax
from jax.experimental import pallas as pl
from jax.experimental.pallas import tpu as pltpu
from jax.sharding import PartitionSpec as P

STEP_SIZE = 0.4
B = 128
MESH = pl.DeviceIdType.MESH
F32 = jnp.float32
BF16 = jnp.bfloat16
REACH = {1: (0,), 2: (0, 1), 4: (2, 1, -1, 0)}


def split(value):
    high = value.astype(BF16)
    return high, (value - high.astype(F32)).astype(BF16)


def product(left, right):
    dot = functools.partial(jnp.dot, preferred_element_type=F32)
    return dot(left[0], right[0]) + (dot(left[0], right[1]) + dot(left[1], right[0]))


def block(index):
    return pl.ds(index * B, B)


def kernel(
    n_row,
    n_col,
    source_ref,
    out_ref,
    pos_ref,
    quad,
    half_done,
    turned,
    parts,
    arrived,
    gen,
    full,
    rows_high,
    rows_low,
    cols_high,
    cols_low,
    done,
    landed,
    turn_rows,
    tri_out,
    tri_in,
    centre_out,
    centre_in,
    load_sem,
    keep_sem,
    ready,
    swap_send,
    swap_recv,
    raw_send,
    raw_recv,
    piece_send,
    piece_recv,
    f_send,
    f_recv,
    p_send,
    p_recv,
    y_send,
    y_recv,
    r_send,
    r_recv,
    a_send,
    a_recv,
    b_send,
    b_recv,
    z_send,
    z_recv,
):
    n_quad = n_col // 4
    row = lax.axis_index("row")
    col = lax.axis_index("col")
    row_quad, upper = lax.rem(row, n_quad), lax.div(row, n_quad)
    col_high, low = lax.div(col, n_col // 2), lax.rem(col, 2)
    col_quad = lax.div(lax.rem(col, n_col // 2), 2)
    mine = 2 * col_high + low
    on_diagonal = row_quad == col_quad
    off_diagonal = row_quad != col_quad
    owner = jnp.logical_and(on_diagonal, upper == col_high)
    guest = jnp.logical_and(on_diagonal, upper != col_high)
    first_owner = jnp.logical_and(owner, low == 0)
    second_owner = jnp.logical_and(owner, low == 1)
    core = lax.rem(row, 2)
    sibling = (row + 1 - 2 * core, col)
    leader = jnp.logical_and(off_diagonal, core == lax.rem(col_quad, 2))
    follower = core != lax.rem(col_quad, 2)
    far_row = lax.rem(row + n_quad, n_row)

    def column(quad_id, place):
        return (n_col // 2) * lax.div(place, 2) + 2 * quad_id + lax.rem(place, 2)

    def peer(step):
        place = 2 * (1 - col_high if step >= 2 else col_high) + (1 - low if step % 2 else low)
        return place, (row, column(col_quad, place))

    def sender(step):
        return peer(step)[0]

    def remote(src, dst, send, recv, device):
        return pltpu.make_async_remote_copy(
            src_ref=src, dst_ref=dst, send_sem=send, recv_sem=recv, device_id=device, device_id_type=MESH
        )

    reach = REACH[n_row // 4]
    hops = sorted(range(1, n_quad), key=lambda hop: abs(hop % 4 - 2))
    row_targets = [(row, column(lax.rem(row_quad + hop, n_quad), mine)) for hop in hops]
    chip = lax.div(row, 2)
    n_chip = n_row // 2

    def above(hop):
        return 2 * lax.rem(chip + n_chip + hop, n_chip) + core, col

    col_targets = [above(hop) for hop in reach if hop != 0]
    other_targets = [above(n_chip // 2 + hop) for hop in reach if hop != 0]
    col_hops = [hop % n_chip for hop in reach if hop != 0] + [(n_chip // 2 + hop) % n_chip for hop in reach if hop != 0]
    far_first = sorted(range(len(col_hops)), key=lambda number: -min(col_hops[number], n_chip - col_hops[number]))
    row_source = (row, column(row_quad, mine))
    away = lax.rem(chip + n_row // 2 - lax.div(col_quad, 2), n_row // 2)
    wraps = lax.div(away + n_row // 8 - (1 if n_row >= 16 else 0), n_row // 4) if n_row >= 16 else lax.div(away, n_row // 4)
    col_source = (lax.rem(col_quad + n_quad * lax.rem(wraps, 2), n_row), col)
    col_owner = (col_quad + n_quad * col_high, col)
    near_owner = jnp.logical_and(leader, lax.rem(wraps, 2) == col_high)
    far_owner = jnp.logical_and(leader, lax.rem(wraps, 2) != col_high)

    load = pltpu.make_async_copy(source_ref, pos_ref, load_sem)
    load.start()

    barrier = pltpu.get_barrier_semaphore()

    def greet(device):
        pl.semaphore_signal(barrier, inc=1, device_id=device, device_id_type=MESH)

    @pl.when(on_diagonal)
    def _():
        for side in (0, 1):
            greet((far_row, column(col_quad, 2 * (1 - upper) + side)))

    for step in (1, 2, 3):
        greet((row, column(col_quad, sender(step))))

    @pl.when(off_diagonal)
    def _():
        greet((far_row, col))

    @pl.when(follower)
    def _():
        greet(sibling)

    @pl.when(on_diagonal)
    def _():
        for device in row_targets + col_targets:
            greet(device)

    @pl.when(owner)
    def _():
        for device in other_targets:
            greet(device)

    def answer(device):
        pl.semaphore_signal(ready, inc=1, device_id=device, device_id_type=MESH)

    @pl.when(follower)
    def _():
        pl.semaphore_wait(barrier, 3 + 1 + 1)
        answer(row_source)

    @pl.when(near_owner)
    def _():
        pl.semaphore_wait(barrier, 3 + 1 + 2 + 1)
        answer(row_source)
        answer(col_source)

    @pl.when(far_owner)
    def _():
        pl.semaphore_wait(barrier, 3 + 1 + 3 + 1)
        answer(row_source)
        answer(col_source)
        answer(col_owner)

    @pl.when(owner)
    def _():
        pl.semaphore_wait(barrier, 3 + 4 + 1)

    @pl.when(guest)
    def _():
        pl.semaphore_wait(barrier, 3 + 1)

    load.wait()

    own_rows = pl.ds(pl.multiple_of(upper * 2 * B, 2 * B), 2 * B)
    far_rows = pl.ds(pl.multiple_of((1 - upper) * 2 * B, 2 * B), 2 * B)

    def lanes(place):
        return pl.ds(pl.multiple_of(place * B, B), B)

    def share(step):
        place, device = peer(step)
        return remote(
            pos_ref.at[place], quad.at[own_rows, lanes(mine)], p_send.at[step - 1], p_recv.at[step - 1], device
        )

    def raw(place):
        return remote(
            pos_ref.at[place],
            quad.at[own_rows, lanes(mine)],
            raw_send.at[place],
            raw_recv.at[low],
            (far_row, column(col_quad, place)),
        )

    row_ids = lax.broadcasted_iota(jnp.int32, (B, B), 0)
    col_ids = lax.broadcasted_iota(jnp.int32, (B, B), 1)

    def reduce_copy(turn, step):
        place, device = peer(step)
        return remote(
            parts.at[turn, place],
            arrived.at[turn, step - 1],
            r_send.at[turn, step - 1],
            r_recv.at[turn, step - 1],
            device,
        )

    def serve_copy(turn, kind, number):
        device = (row_targets if kind == 0 else col_targets + other_targets)[number]
        slot = number + kind * len(row_targets)
        return remote(
            gen.at[turn, 0, mine], gen.at[turn, kind, mine], a_send.at[turn, slot], a_recv.at[turn, kind], device
        )

    def gather_copy(turn, kind, step):
        _, device = peer(step)
        return remote(
            gen.at[turn, kind, mine],
            gen.at[turn, kind, mine],
            b_send.at[turn, kind, step - 1],
            b_recv.at[turn, kind, step - 1],
            device,
        )

    def gather_wait(turn, kind, step):
        place = sender(step)
        _, device = peer(step)
        remote(
            gen.at[turn, kind, place],
            gen.at[turn, kind, place],
            b_send.at[turn, kind, step - 1],
            b_recv.at[turn, kind, step - 1],
            device,
        ).wait_recv()

    def centre(tile):
        kept = jnp.where(row_ids == col_ids, tile, 0.0)
        return jnp.sum(kept, axis=0, keepdims=True), jnp.sum(kept, axis=1, keepdims=True)

    partner = (row, column(col_quad, mine + 1 - 2 * low))
    here = gen.at[0, 0, mine]
    piece = remote(here, here, piece_send, piece_recv, (far_row, col))
    give_tri = remote(tri_out, tri_in, swap_send, swap_recv, partner)
    give_centre = remote(centre_out, centre_in, swap_send, swap_recv, partner)

    @pl.when(second_owner)
    def _():
        total = jnp.zeros((B, B), F32)
        for matrix in range(4):
            tile = pos_ref[matrix, B:]
            across, down = centre(tile)
            centre_out[matrix : matrix + 1] = across
            total = total + tile * (across - down)
        give_centre.start()
        tri_out[...] = total

    @pl.when(first_owner)
    def _():
        total = jnp.zeros((B, B), F32)
        for matrix in range(4):
            tile = pos_ref[matrix, :B]
            across, down = centre(tile)
            centre_out[matrix : matrix + 1] = across
            total = total + tile * (across - down)
        tri_out[...] = total
        give_tri.start()

    @pl.when(owner)
    def _():
        for place in range(3):
            raw(place).start()

    for step in (3, 2, 1):
        share(step).start()
    keep = pltpu.make_async_copy(pos_ref.at[mine], quad.at[own_rows, lanes(mine)], keep_sem)
    keep.start()

    @pl.when(second_owner)
    def _():
        give_tri.wait_recv()
        gen[0, 0, mine] = STEP_SIZE * jnp.where(row_ids > col_ids, tri_in[...], tri_out[...])

    @pl.when(first_owner)
    def _():
        give_centre.wait_recv()
        total = jnp.zeros((B, B), F32)
        for matrix in range(4):
            _, down = centre(jnp.broadcast_to(centre_in[matrix : matrix + 1], (B, B)))
            total = total + pos_ref[matrix, B:] * (centre_out[matrix : matrix + 1] - down)
        gen[0, 0, mine] = STEP_SIZE * total

    @pl.when(owner)
    def _():
        piece.start()
        raw(3).start()
        pl.semaphore_wait(ready, len(row_targets) + len(col_targets) + len(other_targets))
        for number in far_first:
            serve_copy(0, 1, number).start()

    def serve_rows(turn):
        for number in range(len(row_targets)):
            serve_copy(turn, 0, number).start()

    def arrive(turn, kind):
        view = gen.at[turn, kind, mine]
        remote(view, view, b_send.at[turn, kind, 0], a_recv.at[turn, kind], row_source).wait_recv()
        for step in (3, 2, 1):
            gather_copy(turn, kind, step).start()

    def hand(turn, step, kind):
        place = mine if step == 0 else sender(step)
        return remote(
            gen.at[turn, kind, place], gen.at[turn, 1, place], f_send.at[turn, step], f_recv.at[turn, step], sibling
        )

    def pass_on_column(turn):
        @pl.when(leader)
        def _():
            arrive(turn, 1)
            hand(turn, 0, 1).start()

    @pl.when(guest)
    def _():
        piece.wait_recv()

    @pl.when(on_diagonal)
    def _():
        for step in (3, 2, 1):
            gather_copy(0, 0, step).start()

    @pl.when(guest)
    def _():
        pl.semaphore_wait(ready, len(row_targets) + len(col_targets))

    @pl.when(on_diagonal)
    def _():
        serve_rows(0)

    @pl.when(owner)
    def _():
        for number in far_first:
            serve_copy(0, 1, number).wait_send()

    @pl.when(on_diagonal)
    def _():
        hand(0, 0, 0).start()

    def cross(step):
        place = mine if step == 0 else sender(step)
        view = quad.at[own_rows, lanes(place)]
        return remote(pos_ref.at[mine] if step == 0 else view, view, y_send.at[step], y_recv.at[step], (far_row, col))

    def crossed(step):
        view = quad.at[far_rows, lanes(mine if step == 0 else sender(step))]
        return remote(view, view, y_send.at[step], y_recv.at[step], (far_row, col))

    def shared(step):
        view = quad.at[own_rows, lanes(sender(step))]
        return remote(pos_ref.at[0], view, p_send.at[step - 1], p_recv.at[step - 1], peer(step)[1])

    @pl.when(off_diagonal)
    def _():
        for step in (1, 2, 3):
            shared(step).wait_recv()

    @pl.when(on_diagonal)
    def _():
        for step in (1, 2, 3):
            shared(step).wait_recv()

    keep.wait()

    pass_on_column(0)

    @pl.when(follower)
    def _():
        hand(0, 0, 1).wait_recv()

    @pl.when(off_diagonal)
    def _():
        for step in range(2):
            cross(step).start()
        arrive(0, 0)
        for step in range(2, 4):
            crossed(step - 2).wait_recv()
            cross(step).start()

    def span(side, number):
        return pl.ds(pl.multiple_of((2 * side + number) * B, B), B)

    @pl.when(on_diagonal)
    def _():
        for far in (0, 1):
            for near in (0, 1):
                there, back = span(1 - upper, far), span(upper, near)
                quad[there, back] = quad[back, there].T

    def make_parts(source, turn):
        for pair in (0, 1):
            first, second = block(2 * pair), block(2 * pair + 1)
            head, tail = source[first, first], source[second, second]
            same = row_ids == col_ids
            head_kept, tail_kept = jnp.where(same, head, 0.0), jnp.where(same, tail, 0.0)
            head_across = jnp.sum(head_kept, axis=0, keepdims=True)
            tail_across = jnp.sum(tail_kept, axis=0, keepdims=True)
            head_down = jnp.sum(head_kept, axis=1, keepdims=True)
            tail_down = jnp.sum(tail_kept, axis=1, keepdims=True)
            parts[turn, 2 * pair] = source[second, first] * (head_across - tail_down)
            parts[turn, 2 * pair + 1] = jnp.where(
                row_ids > col_ids, head * (head_across - head_down), tail * (tail_across - tail_down)
            )

    def distribute(source, turn):
        @pl.when(on_diagonal)
        def _():
            make_parts(source, turn)
            for step in (3, 2, 1):
                reduce_copy(turn, step).start()
            total = parts[turn, mine]
            for step in (1, 2, 3):
                remote(
                    parts.at[turn, 0],
                    arrived.at[turn, step - 1],
                    r_send.at[turn, step - 1],
                    r_recv.at[turn, step - 1],
                    peer(step)[1],
                ).wait_recv()
                total = total + arrived[turn, step - 1]
            gen[turn, 0, mine] = STEP_SIZE * total
            for number in range(len(col_targets)):
                serve_copy(turn, 1, number).start()
            serve_rows(turn)
            for step in (3, 2, 1):
                gather_copy(turn, 0, step).start()

    identity = jnp.where(
        lax.broadcasted_iota(jnp.int32, (2 * B, 2 * B), 0) == lax.broadcasted_iota(jnp.int32, (2 * B, 2 * B), 1),
        1.0,
        0.0,
    ).astype(F32)

    def rotation(turn, kind, pair, sign):
        whole = full.at[pair]
        across = gen[turn, kind, 2 * pair] * sign
        mixed = gen[turn, kind, 2 * pair + 1] * sign
        lower = jnp.where(row_ids > col_ids, mixed, 0.0)
        higher = jnp.where(row_ids < col_ids, mixed, 0.0)
        whole[:B, :B] = lower - lower.T
        whole[B:, B:] = higher - higher.T
        whole[B:, :B] = across
        whole[:B, B:] = -across.T
        once = whole[...]
        halves = split(once)
        twice = product(halves, halves)
        rest = 0.5 * identity + once * (1.0 / 6.0) + twice * (1.0 / 24.0)
        return identity + once + product(split(twice), split(rest))

    def rotations(turn, between):
        for step in (1, 2, 3):
            gather_wait(turn, 0, step)

        @pl.when(on_diagonal)
        def _():
            for step in range(1 if turn == 0 else 0, 4):
                hand(turn, step, 0).start()

        @pl.when(leader)
        def _():
            for step in (1, 2, 3):
                gather_wait(turn, 1, step)
                hand(turn, step, 1).start()

        for pair in (0, 1):
            turn_rows[pair] = rotation(turn, 0, pair, -1.0)
        for pair in (0, 1):
            rows_high[pair], rows_low[pair] = split(turn_rows[pair])

        @pl.when(on_diagonal)
        def _():
            for pair in (0, 1):
                cols_high[pair], cols_low[pair] = split(turn_rows[pair].T)

        between()

        @pl.when(follower)
        def _():
            for step in range(1 if turn == 0 else 0, 4):
                hand(turn, step, 1).wait_recv()

        @pl.when(off_diagonal)
        def _():
            for pair in (0, 1):
                cols_high[pair], cols_low[pair] = split(rotation(turn, 1, pair, 1.0))

    rotations(0, lambda: None)

    @pl.when(on_diagonal)
    def _():
        for side in (0, 1):
            remote(
                pos_ref.at[0],
                quad.at[far_rows, lanes(2 * (1 - upper) + side)],
                raw_send.at[side],
                raw_recv.at[side],
                (far_row, col),
            ).wait_recv()

    @pl.when(off_diagonal)
    def _():
        arrive(1, 0)

    pass_on_column(1)

    @pl.when(off_diagonal)
    def _():
        for step in range(2, 4):
            crossed(step).wait_recv()

    for pair in (0, 1):
        moved = product(split(quad[:, pl.ds(pair * 2 * B, 2 * B)]), (cols_high[pair], cols_low[pair]))
        half_done[:, block(pair)] = moved[:, :B]
        half_done[:, block(pair + 2)] = moved[:, B:]
    for pair in (0, 1):
        moved = product((rows_high[pair], rows_low[pair]), split(half_done[pl.ds(pair * 2 * B, 2 * B), :]))
        turned[block(pair), :] = moved[:B]
        turned[block(pair + 2), :] = moved[B:]

    distribute(turned, 1)
    half = pl.ds(pl.multiple_of(upper * B, B), B)

    def left_products():
        for part in (0, 1):
            half_done[block(part), :] = product(
                (rows_high[part, half], rows_low[part, half]), split(turned[pl.ds(part * 2 * B, 2 * B), :])
            )

    rotations(1, left_products)

    def give_back(part, step):
        place, device = peer(step)
        return remote(
            done.at[place, block(part)],
            landed.at[mine, block(part)],
            z_send.at[part, step - 1],
            z_recv.at[part, step - 1],
            device,
        )

    for part in (0, 1):
        for pair in (0, 1):
            moved = half_done[block(part), pl.ds(pair * 2 * B, 2 * B)]
            final = product(split(moved), (cols_high[pair], cols_low[pair]))
            done[pair, block(part)] = final[:, :B]
            done[pair + 2, block(part)] = final[:, B:]
        for step in (3, 2, 1):
            give_back(part, step).start()
    out_ref[mine] = done[mine]
    for part in (0, 1):
        for step in (1, 2, 3):
            place = sender(step)
            remote(
                done.at[0, block(part)],
                landed.at[place, block(part)],
                z_send.at[part, step - 1],
                z_recv.at[part, step - 1],
                peer(step)[1],
            ).wait_recv()
            out_ref[place, block(part)] = landed[place, block(part)]

    for step in (1, 2, 3):
        share(step).wait_send()
    for part in (0, 1):
        for step in (1, 2, 3):
            give_back(part, step).wait_send()
    for turn in (0, 1):
        for step in (1, 2, 3):
            gather_copy(turn, 0, step).wait_send()

        @pl.when(on_diagonal)
        def _():
            if turn == 1:
                for step in (1, 2, 3):
                    reduce_copy(turn, step).wait_send()
                for number in range(len(col_targets)):
                    serve_copy(turn, 1, number).wait_send()
            for number in range(len(row_targets)):
                serve_copy(turn, 0, number).wait_send()

            for step in range(4):
                hand(turn, step, 0).wait_send()

        @pl.when(leader)
        def _():
            for step in (1, 2, 3):
                gather_copy(turn, 1, step).wait_send()
            for step in range(4):
                hand(turn, step, 1).wait_send()

        @pl.when(off_diagonal)
        def _():
            if turn == 0:
                for step in range(4):
                    cross(step).wait_send()

    @pl.when(first_owner)
    def _():
        give_tri.wait_send()

    @pl.when(second_owner)
    def _():
        give_centre.wait_send()

    @pl.when(owner)
    def _():
        piece.wait_send()
        for place in range(4):
            raw(place).wait_send()


def local(n_row, n_col, positions):
    dma = pltpu.SemaphoreType.DMA
    n_serve = n_col // 4 - 1 + 2 * (n_row // 4 - 1)
    return pl.pallas_call(
        functools.partial(kernel, n_row, n_col),
        out_shape=jax.ShapeDtypeStruct(positions.shape, F32),
        in_specs=[pl.BlockSpec(memory_space=pltpu.HBM)],
        out_specs=pl.BlockSpec(memory_space=pltpu.VMEM),
        scratch_shapes=[
            pltpu.VMEM((4, 2 * B, B), F32),
            pltpu.VMEM((4 * B, 4 * B), F32),
            pltpu.VMEM((4 * B, 4 * B), F32),
            pltpu.VMEM((4 * B, 4 * B), F32),
            pltpu.VMEM((2, 4, B, B), F32),
            pltpu.VMEM((2, 3, B, B), F32),
            pltpu.VMEM((2, 2, 4, B, B), F32),
            pltpu.VMEM((2, 2 * B, 2 * B), F32),
            pltpu.VMEM((2, 2 * B, 2 * B), BF16),
            pltpu.VMEM((2, 2 * B, 2 * B), BF16),
            pltpu.VMEM((2, 2 * B, 2 * B), BF16),
            pltpu.VMEM((2, 2 * B, 2 * B), BF16),
            pltpu.VMEM((4, 2 * B, B), F32),
            pltpu.VMEM((4, 2 * B, B), F32),
            pltpu.VMEM((2, 2 * B, 2 * B), F32),
            pltpu.VMEM((B, B), F32),
            pltpu.VMEM((B, B), F32),
            pltpu.VMEM((8, B), F32),
            pltpu.VMEM((8, B), F32),
            dma,
            dma,
            pltpu.SemaphoreType.REGULAR,
            dma,
            dma,
            dma((4,)),
            dma((2,)),
            dma,
            dma,
            dma((2, 4)),
            dma((2, 4)),
            dma((3,)),
            dma((3,)),
            dma((4,)),
            dma((4,)),
            dma((2, 3)),
            dma((2, 3)),
            dma((2, n_serve)),
            dma((2, 2)),
            dma((2, 2, 3)),
            dma((2, 2, 3)),
            dma((2, 3)),
            dma((2, 3)),
        ],
        compiler_params=pltpu.CompilerParams(collective_id=0, has_side_effects=True, vmem_limit_bytes=48 * 2**20),
    )(pltpu.with_memory_space_constraint(positions, pltpu.HBM))


def solution(mesh):
    body = functools.partial(local, mesh.shape["row"], mesh.shape["col"])
    spec = P(None, "row", "col")
    return jax.shard_map(body, mesh=mesh, in_specs=(spec,), out_specs=spec, check_vma=False)
```
